32 devices in a mesh: fsdp: 8 (over y, x, core), mode: 4 (over z).
Axes of the slice: x: 2, y: 2, z: 4, core: 2. Of those that a mesh axis runs over, the one named last changes fastest.
Arguments:
- gradient: float32 [32, 16, 2, 256, 512], P('mode', None, None, 'fsdp'), may hold values from -1000 to 1000, as said below
- start_in: float32 [512, 128], replicated, may hold values from -6 to 6
- start_out: float32 [256, 128], replicated, may hold values from -6 to 6
- start_x: float32 [32, 16], replicated, may hold values from -6 to 6
- start_y: float32 [16, 8], replicated, may hold values from -6 to 6
Outputs:
- factor_in: float32 [512, 128], P(('fsdp', 'mode'))
- factor_out: float32 [256, 128], P('fsdp')
- factor_x: float32 [32, 16], replicated
- factor_y: float32 [16, 8], replicated
- core: float32 [16, 128, 8, 2, 128], P('mode', 'fsdp')
The draws below stay inside these ranges and needn't reach their ends.
Inputs may be any that keep to these rules, and one draw needn't show every extreme that they name: A weight gradient of one spectral layer, finite and bounded in magnitude.
All inputs are finite; a program needn't handle non-finite values.
Results may differ from the reference program's by a relative error of at most 0.0003.
Values sent between devices are 32-bit elements; how exact they have to be, the bound alone decides.
No kernel may reach another device: no remote copies, remote signals or barrier semaphores. Data moves between devices by JAX's collectives and lax.ppermute only.
A program may use at most 320 MiB of HBM per device.

```python
import math
import jax
import jax.numpy as jnp
from jax import lax

I = 512
O = 256
X = 32
Y = 16
C = 2
RI = 128
RO = 128
RX = 16
RY = 8
SWEEPS = 2


def draw_gradient(key, part):
    subkeys = jax.random.split(key, 11)
    full_shape = (X, Y, C, O, I)
    rise = math.log(3.0)
    scale_in = jnp.exp(jax.random.uniform(subkeys[0], (I,), jnp.float32, 0.0, math.log(3.2)))
    scale_out = jnp.exp(rise * jnp.arange(O, dtype=jnp.float32) / O + jax.random.uniform(subkeys[1], (O,), jnp.float32, 0.0, 0.7))
    scale_first = jnp.exp(rise * jnp.arange(X, dtype=jnp.float32) / X + jax.random.uniform(subkeys[2], (X,), jnp.float32, 0.0, 0.7))
    scale_second = jnp.exp(jax.random.uniform(subkeys[3], (Y,), jnp.float32, 0.0, 0.7))
    profile_first = jax.random.uniform(subkeys[7], (2, X), jnp.float32, -1.0, 1.0)
    profile_second = jax.random.uniform(subkeys[8], (2, Y), jnp.float32, -1.0, 1.0)
    field_first = jnp.clip(jax.random.normal(subkeys[9], (2, Y, C, O, I), jnp.float32), -3.0, 3.0)
    field_second = jnp.clip(jax.random.normal(subkeys[10], (2, X, C, O, I), jnp.float32), -3.0, 3.0)
    shared = profile_first[0][:, None, None, None, None] * field_first[0][None]
    shared = shared + profile_first[1][:, None, None, None, None] * field_first[1][None]
    shared = shared + profile_second[0][None, :, None, None, None] * field_second[0][:, None]
    shared = shared + profile_second[1][None, :, None, None, None] * field_second[1][:, None]
    fluctuation = jnp.clip(jax.random.normal(subkeys[4], full_shape, jnp.float32), -4.0, 4.0)
    fluctuation = fluctuation + shared
    scaling = scale_first[:, None, None, None, None] * scale_second[None, :, None, None, None]
    scaling = scaling * scale_out[None, None, None, :, None] * scale_in[None, None, None, None, :]
    return jnp.clip(fluctuation * scaling, -1000.0, 1000.0)


def bell_draw(own_key, dims, spread, reach, kind=jnp.bfloat16):
    entries = spread * jax.random.normal(own_key, dims, jnp.float32)
    return jnp.clip(entries, min=-reach, max=reach).astype(kind)


def setup_inputs(seed: int = 0) -> dict:
    streams_of = jax.random.split(jax.random.key(seed), 6)
    return {
        "gradient": draw_gradient(jax.random.fold_in(streams_of[5], 71), 0),
        "start_in": bell_draw(streams_of[1], (I, RI), 1.0, 6.0, jnp.float32),
        "start_out": bell_draw(streams_of[2], (O, RO), 1.0, 6.0, jnp.float32),
        "start_x": bell_draw(streams_of[3], (X, RX), 1.0, 6.0, jnp.float32),
        "start_y": bell_draw(streams_of[4], (Y, RY), 1.0, 6.0, jnp.float32),
    }


precise = lax.Precision.HIGHEST

def sweeps(gram, subspace):
    for sweep_index in range(SWEEPS):
        product = jnp.dot(gram, subspace, precision=precise)
        inner = jnp.dot(product.T, product, precision=precise)
        lower_factor = jnp.linalg.cholesky(inner)
        subspace = jax.scipy.linalg.solve_triangular(lower_factor, product.T, lower=True).T
    return subspace

def reference(gradient, start_in, start_out, start_x, start_y):
    gram_in = jnp.einsum('xycoi,xycoj->ij', gradient, gradient, precision=precise)
    gram_out = jnp.einsum('xycoi,xycpi->op', gradient, gradient, precision=precise)
    gram_x = jnp.einsum('xycoi,zycoi->xz', gradient, gradient, precision=precise)
    gram_y = jnp.einsum('xycoi,xzcoi->yz', gradient, gradient, precision=precise)
    factor_in = sweeps(gram_in, start_in)
    factor_out = sweeps(gram_out, start_out)
    factor_x = sweeps(gram_x, start_x)
    factor_y = sweeps(gram_y, start_y)
    reduced = jnp.einsum('xycoi,ia->xycoa', gradient, factor_in, precision=precise)
    reduced = jnp.einsum('xycoa,yq->xqcoa', reduced, factor_y, precision=precise)
    reduced = jnp.einsum('xqcoa,ob->xbqca', reduced, factor_out, precision=precise)
    core = jnp.einsum('xbqca,xp->pbqca', reduced, factor_x, precision=precise)
    return (factor_in, factor_out, factor_x, factor_y, core)
```

```python
import jax
import jax.numpy as jnp
from jax import lax
from jax.experimental import pallas as pl
from jax.experimental.pallas import tpu as pltpu
from jax.sharding import PartitionSpec as P

SWEEPS = 2
ROWS = 8

precise = lax.Precision.HIGHEST
F32 = jnp.float32
BF16 = jnp.bfloat16


def split(a):
    high = a.astype(BF16)
    low = (a - high.astype(F32)).astype(BF16)
    return high, low


def dot_nt(a, b):
    return lax.dot_general(a, b, (((1,), (1,)), ((), ())), preferred_element_type=F32)


def dot_nn(a, b):
    return jnp.dot(a, b, preferred_element_type=F32)


def dot_tn(a, b):
    return lax.dot_general(a, b, (((0,), (0,)), ((), ())), preferred_element_type=F32)


def exact_nn(a, b):
    return lax.dot_general(
        a, b, (((1,), (0,)), ((), ())), precision=precise, preferred_element_type=F32
    )


def exact_nt(a, b):
    return lax.dot_general(
        a, b, (((1,), (1,)), ((), ())), precision=precise, preferred_element_type=F32
    )


def symmetric(acc, n):
    cross = acc[:, n:]
    return acc[:, :n] + cross + cross.T


def rows_gram(a):
    high, low = split(a)
    return dot_nt(high, jnp.concatenate([high, low], axis=0))


def same_row(n):
    r = lax.broadcasted_iota(jnp.int32, (n, n), 0)
    c = lax.broadcasted_iota(jnp.int32, (n, n), 1)
    return (r & (ROWS - 1)) == (c & (ROWS - 1))


def group_select(n, group, place=lambda k: k):
    r = lax.broadcasted_iota(jnp.int32, (n // group, n), 0)
    c = lax.broadcasted_iota(jnp.int32, (n // group, n), 1)
    return jnp.where(r == place(c // group), 1.0, 0.0).astype(F32)


def gram_y_kernel(g_ref, o_ref, acc_ref):
    _, ny, nc, no, ni = g_ref.shape
    n = ny * ROWS

    @pl.when(pl.program_id(0) == 0)
    def _():
        acc_ref[...] = jnp.zeros_like(acc_ref)

    for c in range(nc):
        for t in range(no // ROWS):
            a = g_ref[0, :, c, t * ROWS : (t + 1) * ROWS, :].reshape(n, ni)
            acc_ref[...] += rows_gram(a)

    @pl.when(pl.program_id(0) == pl.num_programs(0) - 1)
    def _():
        full = jnp.where(same_row(n), symmetric(acc_ref[...], n), 0.0)
        select = group_select(n, ROWS)
        o_ref[...] = exact_nt(exact_nn(select, full), select)


def gram_y_part(gradient):
    nx, ny, nc, no, ni = gradient.shape
    return pl.pallas_call(
        gram_y_kernel,
        grid=(nx,),
        in_specs=[pl.BlockSpec((1, ny, nc, no, ni), lambda x: (x, 0, 0, 0, 0))],
        out_specs=pl.BlockSpec((ny, ny), lambda x: (0, 0)),
        out_shape=jax.ShapeDtypeStruct((ny, ny), F32),
        scratch_shapes=[pltpu.VMEM((ny * ROWS, 2 * ny * ROWS), F32)],
        name="gram_y",
    )(gradient)


def gram_x_part(own, base, received, place, prev):
    nx, count, no, ni = received[0].shape
    sources = len(received) + 1
    total = sources * nx
    n = total * ROWS

    def kernel(s_ref, own_ref, *refs):
        parts = (own_ref,) + refs[: sources - 1]
        prev_ref, o_ref, acc_ref = refs[sources - 1 :]

        @pl.when(pl.program_id(0) == 0)
        def _():
            acc_ref[...] = jnp.zeros_like(acc_ref)

        for t in range(no // ROWS):
            a = jnp.concatenate(
                [r[:, 0, t * ROWS : (t + 1) * ROWS, :].reshape(nx * ROWS, ni) for r in parts], axis=0
            )
            acc_ref[...] += rows_gram(a)

        @pl.when(pl.program_id(0) == pl.num_programs(0) - 1)
        def _():
            full = jnp.where(same_row(n), symmetric(acc_ref[...], n), 0.0)
            mine = s_ref[1]
            select = group_select(n, ROWS, lambda k: ((k // nx) ^ mine) * nx + k % nx)
            o_ref[...] = prev_ref[...] + exact_nt(exact_nn(select, full), select)

    grid_spec = pltpu.PrefetchScalarGridSpec(
        num_scalar_prefetch=1,
        grid=(count,),
        in_specs=[pl.BlockSpec((nx, 1, no, ni), lambda u, s: (0, s[0] + u, 0, 0))]
        + [pl.BlockSpec((nx, 1, no, ni), lambda u, s: (0, u, 0, 0))] * (sources - 1)
        + [pl.BlockSpec((total, total), lambda u, s: (0, 0))],
        out_specs=pl.BlockSpec((total, total), lambda u, s: (0, 0)),
        scratch_shapes=[pltpu.VMEM((n, 2 * n), F32)],
    )
    scalars = jnp.stack([base, place]).astype(jnp.int32)
    return pl.pallas_call(
        kernel,
        grid_spec=grid_spec,
        out_shape=jax.ShapeDtypeStruct((total, total), F32),
        name="gram_x",
    )(scalars, own, *received, prev)


def gram_out_part(own, base, received, place, prev):
    nx, count, no, ni = received[0].shape
    sources = len(received) + 1
    n = sources * no

    def kernel(s_ref, own_ref, *refs):
        parts = (own_ref,) + refs[: sources - 1]
        prev_ref, o_ref, acc_ref = refs[sources - 1 :]
        step = pl.program_id(0) * pl.num_programs(1) + pl.program_id(1)

        @pl.when(step == 0)
        def _():
            acc_ref[...] = jnp.zeros_like(acc_ref)

        acc_ref[...] += rows_gram(jnp.concatenate([r[0, 0] for r in parts], axis=0))

        @pl.when(step == pl.num_programs(0) * pl.num_programs(1) - 1)
        def _():
            mine = s_ref[1]
            r = lax.broadcasted_iota(jnp.int32, (n, n), 0)
            c = lax.broadcasted_iota(jnp.int32, (n, n), 1)
            select = jnp.where(r == ((c // no) ^ mine) * no + c % no, 1.0, 0.0).astype(F32)
            full = symmetric(acc_ref[...], n)
            o_ref[...] = prev_ref[...] + exact_nt(exact_nn(select, full), select)

    grid_spec = pltpu.PrefetchScalarGridSpec(
        num_scalar_prefetch=1,
        grid=(nx, count),
        in_specs=[pl.BlockSpec((1, 1, no, ni), lambda x, u, s: (x, s[0] + u, 0, 0))]
        + [pl.BlockSpec((1, 1, no, ni), lambda x, u, s: (x, u, 0, 0))] * (sources - 1)
        + [pl.BlockSpec((n, n), lambda x, u, s: (0, 0))],
        out_specs=pl.BlockSpec((n, n), lambda x, u, s: (0, 0)),
        scratch_shapes=[pltpu.VMEM((n, 2 * n), F32)],
    )
    scalars = jnp.stack([base, place]).astype(jnp.int32)
    return pl.pallas_call(
        kernel,
        grid_spec=grid_spec,
        out_shape=jax.ShapeDtypeStruct((n, n), F32),
        name="gram_out",
    )(scalars, own, *received, prev)


def project(own, base, received, factor_in, factor_out):
    nx, count, no, ni = received[0].shape
    sources = len(received) + 1
    n = sources * no
    ra = factor_in.shape[1]
    rb = factor_out.shape[1]

    def kernel(s_ref, own_ref, *refs):
        parts = (own_ref,) + refs[: sources - 1]
        in_ref, out_ref, v_ref = refs[sources - 1 :]
        high, low = split(jnp.concatenate([r[0, 0] for r in parts], axis=0))
        in_high, in_low = split(in_ref[...])
        u = dot_nn(high, in_high) + (dot_nn(high, in_low) + dot_nn(low, in_high))
        u_high, u_low = split(u)
        out_high, out_low = split(out_ref[...])
        v = dot_tn(out_high, u_high) + (dot_tn(out_high, u_low) + dot_tn(out_low, u_high))
        v_ref[0, 0] = v

    grid_spec = pltpu.PrefetchScalarGridSpec(
        num_scalar_prefetch=1,
        grid=(nx, count),
        in_specs=[pl.BlockSpec((1, 1, no, ni), lambda x, u, s: (x, s[0] + u, 0, 0))]
        + [pl.BlockSpec((1, 1, no, ni), lambda x, u, s: (x, u, 0, 0))] * (sources - 1)
        + [
            pl.BlockSpec((ni, ra), lambda x, u, s: (0, 0)),
            pl.BlockSpec((n, rb), lambda x, u, s: (0, 0)),
        ],
        out_specs=pl.BlockSpec((1, 1, rb, ra), lambda x, u, s: (x, u, 0, 0)),
    )
    return pl.pallas_call(
        kernel,
        grid_spec=grid_spec,
        out_shape=jax.ShapeDtypeStruct((nx, count, rb, ra), F32),
        name="project",
    )(jnp.stack([base]).astype(jnp.int32), own, *received, factor_in, factor_out)


def contract_y(parts, place, factor_y, nc):
    nx, count, nb, na = parts[0].shape
    ny, nq = factor_y.shape
    sources = len(parts)

    def kernel(s_ref, f_ref, *refs):
        o_ref = refs[sources]
        mine = s_ref[0]
        terms = [[[] for _ in range(nc)] for _ in range(nq)]
        for r in range(sources):
            for u in range(count):
                slot = (mine ^ r) * count + u
                y = slot // nc
                value = refs[r][0, u]
                for q in range(nq):
                    scaled = f_ref[y, q] * value
                    for c in range(nc):
                        if count % nc == 0:
                            if u % nc == c:
                                terms[q][c].append(scaled)
                        else:
                            terms[q][c].append(jnp.where(slot % nc == c, scaled, 0.0))
        for q in range(nq):
            for c in range(nc):
                total = terms[q][c][0]
                for term in terms[q][c][1:]:
                    total = total + term
                o_ref[0, q, c] = total

    return pl.pallas_call(
        kernel,
        grid=(nx,),
        in_specs=[
            pl.BlockSpec(memory_space=pltpu.SMEM),
            pl.BlockSpec(memory_space=pltpu.SMEM),
        ]
        + [pl.BlockSpec((1, count, nb, na), lambda x: (x, 0, 0, 0))] * sources,
        out_specs=pl.BlockSpec((1, nq, nc, nb, na), lambda x: (x, 0, 0, 0, 0)),
        out_shape=jax.ShapeDtypeStruct((nx, nq, nc, nb, na), F32),
        name="contract_y",
    )(jnp.stack([place]).astype(jnp.int32), factor_y, *parts)


def contract_x(parts, place, factor_x):
    nx, nq, nc, nb, na = parts[0].shape
    sources = len(parts)
    np_ = factor_x.shape[1] // sources

    def kernel(s_ref, f_ref, *refs):
        o_ref = refs[sources]
        mine = s_ref[0]
        for p in range(np_):
            total = None
            for r in range(sources):
                for x in range(nx):
                    term = f_ref[(mine ^ r) * nx + x, mine * np_ + p] * refs[r][x, 0]
                    total = term if total is None else total + term
            o_ref[p, 0] = total

    return pl.pallas_call(
        kernel,
        grid=(nq,),
        in_specs=[
            pl.BlockSpec(memory_space=pltpu.SMEM),
            pl.BlockSpec(memory_space=pltpu.SMEM),
        ]
        + [pl.BlockSpec((nx, 1, nc, nb, na), lambda q: (0, q, 0, 0, 0))] * sources,
        out_specs=pl.BlockSpec((np_, 1, nc, nb, na), lambda q: (0, q, 0, 0, 0)),
        out_shape=jax.ShapeDtypeStruct((np_, nq, nc, nb, na), F32),
        name="contract_x",
    )(jnp.stack([place]).astype(jnp.int32), factor_x, *parts)


def orthonormal(product):
    inner = jnp.dot(product.T, product, precision=precise)
    lower_factor = jnp.linalg.cholesky(inner)
    return jax.scipy.linalg.solve_triangular(lower_factor, product.T, lower=True).T


def sweeps(gram, subspace):
    for sweep_index in range(SWEEPS):
        subspace = orthonormal(jnp.dot(gram, subspace, precision=precise))
    return subspace


def swap(value, axis, s):
    n = lax.axis_size(axis)
    return lax.ppermute(value, axis, [(i, i ^ s) for i in range(n)])


def block(value, index, size, dim):
    return lax.dynamic_slice_in_dim(value, index * size, size, dim)


def pieces(count, shares):
    runs = []
    start = 0
    total = sum(shares)
    seen = 0
    for share in shares:
        seen += share
        stop = (count * seen) // total
        if stop > start:
            runs.append((start, stop - start))
            start = stop
    return runs


def reduce_rows(partial, extra, f, m):
    nf = lax.axis_size("fsdp")
    nm = lax.axis_size("mode")
    size = partial.shape[0] // nf

    def message(s):
        rows = block(partial, f ^ s, size, 0)
        return rows if extra is None else jnp.concatenate([rows, extra], axis=0)

    with jax.named_scope("rows_fsdp"):
        total = message(0)
        for value in [swap(message(s), "fsdp", s) for s in range(1, nf)]:
            total = total + value
    with jax.named_scope("rows_mode"):
        out = total
        for value in [swap(total, "mode", s) for s in range(1, nm)]:
            out = out + value
    return (out, None) if extra is None else (out[:size], out[size:])


def gather_rows(rows):
    nf = lax.axis_size("fsdp")
    return jnp.concatenate([rows] + [swap(rows, "fsdp", s) for s in range(1, nf)], axis=0)


def relative_rows(value, place, count):
    size = value.shape[0] // count
    return jnp.concatenate([block(value, place ^ s, size, 0) for s in range(count)], axis=0)


def shards(gradient, start_in, start_out, start_x, start_y):
    f = lax.axis_index("fsdp")
    m = lax.axis_index("mode")
    joint = lax.axis_index(("fsdp", "mode"))
    nf = lax.axis_size("fsdp")
    nm = lax.axis_size("mode")
    nx, ny, nc, no, ni = gradient.shape
    slots = ny * nc
    flat = gradient.reshape(nx, slots, no, ni)
    per_mode = slots // nm
    per_fsdp = slots // nf

    def send(axis, place, s, per, run, source):
        part = lax.dynamic_slice(
            source, (0, (place ^ s) * per + run[0], 0, 0), (nx, run[1], no, ni)
        )
        return swap(part, axis, s)

    def exchange(axis, place, count, per, run, after=None):
        source = flat if after is None else lax.optimization_barrier((flat, after))[0]
        return [send(axis, place, s, per, run, source) for s in range(1, count)]

    mode_runs = pieces(per_mode, (1, 3, 3, 1))
    fsdp_runs = pieces(per_fsdp, (1, 1))

    mode_parts = []
    with jax.named_scope("mode_0"):
        mode_parts.append(exchange("mode", m, nm, per_mode, mode_runs[0]))

    with jax.named_scope("gram_in"):
        rows = gradient.reshape(nx * slots * no, ni)
        gram_in_part = lax.dot_general(
            rows, rows, (((0,), (0,)), ((), ())), precision=lax.Precision.HIGH
        )
    with jax.named_scope("gram_y"):
        gram_y = gram_y_part(gradient)
        extra = jnp.pad(gram_y, ((0, (-ny) % ROWS), (0, ni - ny)))
    with jax.named_scope("reduce_in"):
        in_rows, extra = reduce_rows(gram_in_part, extra, f, m)
    gram_y = extra[:ny, :ny]
    with jax.named_scope("mode_1"):
        mode_parts.append(exchange("mode", m, nm, per_mode, mode_runs[1], gram_in_part))
    fsdp_parts = []
    with jax.named_scope("fsdp_0"):
        fsdp_parts.append(exchange("fsdp", f, nf, per_fsdp, fsdp_runs[0], gram_in_part))
    with jax.named_scope("gather_in"):
        gram_in = gather_rows(in_rows)
    for k in range(1, len(fsdp_runs)):
        with jax.named_scope(f"fsdp_{k}"):
            fsdp_parts.append(exchange("fsdp", f, nf, per_fsdp, fsdp_runs[k], in_rows))
    with jax.named_scope("sweeps_in"):
        half = orthonormal(jnp.dot(gram_in, start_in, precision=precise))
        full_in = orthonormal(
            lax.dot_general(gram_in, half, (((0,), (0,)), ((), ())), precision=precise)
        )
    with jax.named_scope("sweeps_y"):
        factor_y = sweeps(gram_y, start_y)

    gram_out = jnp.zeros((nf * no, nf * no), F32)
    with jax.named_scope("gram_out"):
        for run, parts in zip(fsdp_runs, fsdp_parts):
            gram_out = gram_out_part(flat, f * per_fsdp + run[0], parts, f, gram_out)
    with jax.named_scope("reduce_out"):
        out_rows, _ = reduce_rows(gram_out, None, f, m)
    for k in range(2, len(mode_runs)):
        with jax.named_scope(f"mode_{k}"):
            mode_parts.append(exchange("mode", m, nm, per_mode, mode_runs[k], gram_out))
    with jax.named_scope("gather_out"):
        gram_out_full = gather_rows(out_rows)
    with jax.named_scope("sweeps_out"):
        start = relative_rows(start_out, f, nf)
        half = orthonormal(
            lax.dot_general(gram_out_full, start, (((0,), (0,)), ((), ())), precision=precise)
        )
        full_out = orthonormal(jnp.dot(gram_out_full, half, precision=precise))

    with jax.named_scope("project"):
        projected = jnp.concatenate(
            [
                project(flat, f * per_fsdp + run[0], parts, full_in, full_out)
                for run, parts in zip(fsdp_runs, fsdp_parts)
            ],
            axis=1,
        )
    with jax.named_scope("swap_b"):
        nb = projected.shape[2] // nf
        by_b = [block(projected, f, nb, 2)] + [
            swap(block(projected, f ^ s, nb, 2), "fsdp", s) for s in range(1, nf)
        ]
    with jax.named_scope("contract_y"):
        reduced = contract_y(by_b, f, factor_y, nc)

    gram_x = jnp.zeros((nx * nm, nx * nm), F32)
    with jax.named_scope("gram_x"):
        for run, parts in zip(mode_runs, mode_parts):
            gram_x = gram_x_part(flat, m * per_mode + run[0], parts, m, gram_x)
    with jax.named_scope("reduce_x"):
        s = 1
        while s < nf:
            gram_x = gram_x + swap(gram_x, "fsdp", s)
            s *= 2
        s = 1
        while s < nm:
            gram_x = gram_x + swap(gram_x, "mode", s)
            s *= 2
    with jax.named_scope("gather_x"):
        reduced, _ = lax.optimization_barrier((reduced, mode_parts[-1][-1]))
        by_x = [reduced] + [swap(reduced, "mode", s) for s in range(1, nm)]
    with jax.named_scope("sweeps_x"):
        factor_x = sweeps(gram_x, start_x)
    with jax.named_scope("contract_x"):
        core = jnp.transpose(contract_x(by_x, m, factor_x), (0, 3, 1, 2, 4))

    rows_in = ni // (nf * nm)
    factor_in = lax.dynamic_slice_in_dim(full_in, joint * rows_in, rows_in, 0)
    return (factor_in, full_out[:no], factor_x, factor_y, core)


def solution(mesh):
    in_specs = (P("mode", None, None, "fsdp", None), P(), P(), P(), P())
    out_specs = (
        P(("fsdp", "mode"), None),
        P("fsdp", None),
        P(),
        P(),
        P("mode", "fsdp", None, None, None),
    )
    return jax.shard_map(shards, mesh=mesh, in_specs=in_specs, out_specs=out_specs, check_vma=False)
```

```python
import jax
import jax.numpy as jnp
from jax import lax
from jax.experimental import pallas as pl
from jax.experimental.pallas import tpu as pltpu
from jax.sharding import PartitionSpec as P

SWEEPS = 2
ROWS = 8

precise = lax.Precision.HIGHEST
F32 = jnp.float32
BF16 = jnp.bfloat16


def split(a):
    high = a.astype(BF16)
    low = (a - high.astype(F32)).astype(BF16)
    return high, low


def dot_nt(a, b):
    return lax.dot_general(a, b, (((1,), (1,)), ((), ())), preferred_element_type=F32)


def dot_nn(a, b):
    return jnp.dot(a, b, preferred_element_type=F32)


def exact_nn(a, b):
    return lax.dot_general(
        a, b, (((1,), (0,)), ((), ())), precision=precise, preferred_element_type=F32
    )


def exact_nt(a, b):
    return lax.dot_general(
        a, b, (((1,), (1,)), ((), ())), precision=precise, preferred_element_type=F32
    )


def exact_tn(a, b):
    return lax.dot_general(
        a, b, (((0,), (0,)), ((), ())), precision=precise, preferred_element_type=F32
    )


def symmetric(acc, n):
    cross = acc[:, n:]
    return acc[:, :n] + cross + cross.T


def rows_gram(a):
    high, low = split(a)
    return dot_nt(high, jnp.concatenate([high, low], axis=0))


def same_row(n):
    r = lax.broadcasted_iota(jnp.int32, (n, n), 0)
    c = lax.broadcasted_iota(jnp.int32, (n, n), 1)
    return (r & (ROWS - 1)) == (c & (ROWS - 1))


def group_select(n, group, place=lambda k: k):
    r = lax.broadcasted_iota(jnp.int32, (n // group, n), 0)
    c = lax.broadcasted_iota(jnp.int32, (n // group, n), 1)
    return jnp.where(r == place(c // group), 1.0, 0.0).astype(F32)


def gram_y_kernel(g_ref, o_ref, acc_ref):
    _, ny, nc, no, ni = g_ref.shape
    n = ny * ROWS

    @pl.when(pl.program_id(0) == 0)
    def _():
        acc_ref[...] = jnp.zeros_like(acc_ref)

    acc_ref[...] += rows_gram(
        jnp.concatenate(
            [
                g_ref[0, :, c, t * ROWS : (t + 1) * ROWS, :].reshape(n, ni)
                for c in range(nc)
                for t in range(no // ROWS)
            ],
            axis=1,
        )
    )

    @pl.when(pl.program_id(0) == pl.num_programs(0) - 1)
    def _():
        full = jnp.where(same_row(n), symmetric(acc_ref[...], n), 0.0)
        select = group_select(n, ROWS)
        o_ref[...] = exact_nt(exact_nn(select, full), select)


def gram_y_part(gradient):
    nx, ny, nc, no, ni = gradient.shape
    return pl.pallas_call(
        gram_y_kernel,
        grid=(nx,),
        in_specs=[pl.BlockSpec((1, ny, nc, no, ni), lambda x: (x, 0, 0, 0, 0))],
        out_specs=pl.BlockSpec((ny, ny), lambda x: (0, 0)),
        out_shape=jax.ShapeDtypeStruct((ny, ny), F32),
        scratch_shapes=[pltpu.VMEM((ny * ROWS, 2 * ny * ROWS), F32)],
        name="gram_y",
    )(gradient)


def gram_x_part(own, base, received, place, prev):
    nx, count, no, ni = received[0].shape
    sources = len(received) + 1
    total = sources * nx
    n = total * ROWS

    def kernel(s_ref, own_ref, *refs):
        parts = (own_ref,) + refs[: sources - 1]
        prev_ref, o_ref, acc_ref = refs[sources - 1 :]

        @pl.when(pl.program_id(0) == 0)
        def _():
            acc_ref[...] = jnp.zeros_like(acc_ref)

        def rows(t):
            own_rows = [r[:, 0, t * ROWS : (t + 1) * ROWS, :] for r in parts]
            return jnp.concatenate([r.reshape(nx * ROWS, ni) for r in own_rows], axis=0)

        acc_ref[...] += rows_gram(
            jnp.concatenate([rows(t) for t in range(no // ROWS)], axis=1)
        )

        @pl.when(pl.program_id(0) == pl.num_programs(0) - 1)
        def _():
            full = jnp.where(same_row(n), symmetric(acc_ref[...], n), 0.0)
            mine = s_ref[1]
            select = group_select(n, ROWS, lambda k: ((k // nx) ^ mine) * nx + k % nx)
            o_ref[...] = prev_ref[...] + exact_nt(exact_nn(select, full), select)

    grid_spec = pltpu.PrefetchScalarGridSpec(
        num_scalar_prefetch=1,
        grid=(count,),
        in_specs=[pl.BlockSpec((nx, 1, no, ni), lambda u, s: (0, s[0] + u, 0, 0))]
        + [pl.BlockSpec((nx, 1, no, ni), lambda u, s: (0, u, 0, 0))] * (sources - 1)
        + [pl.BlockSpec((total, total), lambda u, s: (0, 0))],
        out_specs=pl.BlockSpec((total, total), lambda u, s: (0, 0)),
        scratch_shapes=[pltpu.VMEM((n, 2 * n), F32)],
    )
    scalars = jnp.stack([base, place]).astype(jnp.int32)
    return pl.pallas_call(
        kernel,
        grid_spec=grid_spec,
        out_shape=jax.ShapeDtypeStruct((total, total), F32),
        name="gram_x",
    )(scalars, own, *received, prev)


def gram_out_part(own, base, received, place, prev):
    nx, count, no, ni = received[0].shape
    sources = len(received) + 1
    n = sources * no

    def kernel(s_ref, own_ref, *refs):
        parts = (own_ref,) + refs[: sources - 1]
        prev_ref, o_ref, acc_ref = refs[sources - 1 :]

        @pl.when(pl.program_id(0) == 0)
        def _():
            acc_ref[...] = jnp.zeros_like(acc_ref)

        acc_ref[...] += rows_gram(
            jnp.concatenate(
                [jnp.concatenate([r[x, 0] for r in parts], axis=0) for x in range(nx)], axis=1
            )
        )

        @pl.when(pl.program_id(0) == pl.num_programs(0) - 1)
        def _():
            mine = s_ref[1]
            r = lax.broadcasted_iota(jnp.int32, (n, n), 0)
            c = lax.broadcasted_iota(jnp.int32, (n, n), 1)
            select = jnp.where(r == ((c // no) ^ mine) * no + c % no, 1.0, 0.0).astype(F32)
            full = symmetric(acc_ref[...], n)
            o_ref[...] = prev_ref[...] + exact_nt(exact_nn(select, full), select)

    grid_spec = pltpu.PrefetchScalarGridSpec(
        num_scalar_prefetch=1,
        grid=(count,),
        in_specs=[pl.BlockSpec((nx, 1, no, ni), lambda u, s: (0, s[0] + u, 0, 0))]
        + [pl.BlockSpec((nx, 1, no, ni), lambda u, s: (0, u, 0, 0))] * (sources - 1)
        + [pl.BlockSpec((n, n), lambda u, s: (0, 0))],
        out_specs=pl.BlockSpec((n, n), lambda u, s: (0, 0)),
        scratch_shapes=[pltpu.VMEM((n, 2 * n), F32)],
    )
    scalars = jnp.stack([base, place]).astype(jnp.int32)
    return pl.pallas_call(
        kernel,
        grid_spec=grid_spec,
        out_shape=jax.ShapeDtypeStruct((n, n), F32),
        name="gram_out",
    )(scalars, own, *received, prev)


def project(own, base, received, factor_in, factor_out):
    nx, count, no, ni = received[0].shape
    sources = len(received) + 1
    n = sources * no
    ra = factor_in.shape[1]
    rb = factor_out.shape[1]

    def kernel(s_ref, own_ref, *refs):
        parts = (own_ref,) + refs[: sources - 1]
        in_ref, out_ref, v_ref = refs[sources - 1 :]
        in_high, in_low = split(in_ref[...])
        in_both = jnp.concatenate([in_high, in_low], axis=1)
        out_high, out_low = split(out_ref[...].T)
        for x in range(nx):
            high, low = split(jnp.concatenate([r[x, 0] for r in parts], axis=0))
            u = dot_nn(high, in_both)
            u = u[:, :ra] + (u[:, ra:] + dot_nn(low, in_high))
            u_high, u_low = split(u)
            v = dot_nn(out_high, jnp.concatenate([u_high, u_low], axis=1))
            v_ref[x, 0] = v[:, :ra] + (v[:, ra:] + dot_nn(out_low, u_high))

    grid_spec = pltpu.PrefetchScalarGridSpec(
        num_scalar_prefetch=1,
        grid=(count,),
        in_specs=[pl.BlockSpec((nx, 1, no, ni), lambda u, s: (0, s[0] + u, 0, 0))]
        + [pl.BlockSpec((nx, 1, no, ni), lambda u, s: (0, u, 0, 0))] * (sources - 1)
        + [
            pl.BlockSpec((ni, ra), lambda u, s: (0, 0)),
            pl.BlockSpec((n, rb), lambda u, s: (0, 0)),
        ],
        out_specs=pl.BlockSpec((nx, 1, rb, ra), lambda u, s: (0, u, 0, 0)),
    )
    return pl.pallas_call(
        kernel,
        grid_spec=grid_spec,
        out_shape=jax.ShapeDtypeStruct((nx, count, rb, ra), F32),
        name="project",
    )(jnp.stack([base]).astype(jnp.int32), own, *received, factor_in, factor_out)


def contract_y(parts, place, factor_y, nc):
    nx, count, nb, na = parts[0].shape
    _, nq = factor_y.shape
    sources = len(parts)

    def kernel(s_ref, f_ref, *refs):
        o_ref = refs[sources]
        mine = s_ref[0]
        terms = [[[] for _ in range(nc)] for _ in range(nq)]
        for r in range(sources):
            for u in range(count):
                slot = (mine ^ r) * count + u
                y = slot // nc
                value = refs[r][0, u]
                for q in range(nq):
                    scaled = f_ref[y, q] * value
                    for c in range(nc):
                        if count % nc == 0:
                            if u % nc == c:
                                terms[q][c].append(scaled)
                        else:
                            terms[q][c].append(jnp.where(slot % nc == c, scaled, 0.0))
        for q in range(nq):
            for c in range(nc):
                total = terms[q][c][0]
                for term in terms[q][c][1:]:
                    total = total + term
                o_ref[0, :, q * nc + c, :] = total

    return pl.pallas_call(
        kernel,
        grid=(nx,),
        in_specs=[
            pl.BlockSpec(memory_space=pltpu.SMEM),
            pl.BlockSpec(memory_space=pltpu.SMEM),
        ]
        + [pl.BlockSpec((1, count, nb, na), lambda x: (x, 0, 0, 0))] * sources,
        out_specs=pl.BlockSpec((1, nb, nq * nc, na), lambda x: (x, 0, 0, 0)),
        out_shape=jax.ShapeDtypeStruct((nx, nb, nq * nc, na), F32),
        name="contract_y",
    )(jnp.stack([place]).astype(jnp.int32), factor_y, *parts)


def contract_x(parts, place, factor_x):
    nx, rows, na = parts[0].shape
    sources = len(parts)
    ranks = factor_x.shape[1]
    step = rows if rows % ROWS else ROWS

    def kernel(s_ref, f_ref, *refs):
        o_ref = refs[sources]
        mine = s_ref[0]
        for t in range(rows // step):
            here = slice(t * step, (t + 1) * step)
            totals = [None] * ranks
            for r in range(sources):
                for x in range(nx):
                    value = refs[r][x, here]
                    for p in range(ranks):
                        term = f_ref[(mine ^ r) * nx + x, p] * value
                        totals[p] = term if totals[p] is None else totals[p] + term
            for p in range(ranks):
                o_ref[p, here] = totals[p]

    return pl.pallas_call(
        kernel,
        in_specs=[
            pl.BlockSpec(memory_space=pltpu.SMEM),
            pl.BlockSpec(memory_space=pltpu.SMEM),
        ]
        + [pl.BlockSpec(memory_space=pltpu.VMEM)] * sources,
        out_specs=pl.BlockSpec(memory_space=pltpu.VMEM),
        out_shape=jax.ShapeDtypeStruct((ranks, rows, na), F32),
        name="contract_x",
    )(jnp.stack([place]).astype(jnp.int32), factor_x, *parts)


def assemble(parts, place):
    sources = len(parts)
    np_, rows, na = parts[0].shape

    def kernel(s_ref, *refs):
        for r in range(sources):
            refs[sources][:, s_ref[0] ^ r] = refs[r][...]

    return pl.pallas_call(
        kernel,
        in_specs=[pl.BlockSpec(memory_space=pltpu.SMEM)]
        + [pl.BlockSpec(memory_space=pltpu.VMEM)] * sources,
        out_specs=pl.BlockSpec(memory_space=pltpu.VMEM),
        out_shape=jax.ShapeDtypeStruct((np_, sources, rows, na), F32),
        name="assemble",
    )(jnp.stack([place]).astype(jnp.int32), *parts)


def splat(value, i, k):
    column = jnp.broadcast_to(value[:, k : k + 1], value.shape)
    return jnp.broadcast_to(column[i : i + 1, :], value.shape)


def inverse_factor(d):
    scale = [None] * ROWS
    lower = [[None] * ROWS for _ in range(ROWS)]
    for k in range(ROWS):
        y = lax.rsqrt(d[k][k])
        scale[k] = y * (1.5 - 0.5 * d[k][k] * y * y)
        for i in range(k + 1, ROWS):
            lower[i][k] = d[i][k] * scale[k]
        for j in range(k + 1, ROWS):
            for i in range(j, ROWS):
                d[i][j] = d[i][j] - lower[i][k] * lower[j][k]
    inverse = [[None] * ROWS for _ in range(ROWS)]
    for k in range(ROWS):
        inverse[k][k] = scale[k]
        for i in range(k + 1, ROWS):
            total = lower[i][k] * inverse[k][k]
            for j in range(k + 1, i):
                total = total + lower[i][j] * inverse[j][k]
            inverse[i][k] = -scale[i] * total
    return inverse


def panel(r, rolled, e):
    row = lax.broadcasted_iota(jnp.int32, r.shape, 0)
    d = [[splat(rolled, i, k) if i >= k else None for k in range(ROWS)] for i in range(ROWS)]
    inverse = inverse_factor(d)
    upper = jnp.zeros_like(r)
    out = jnp.zeros_like(e)
    for k in range(ROWS):
        column = jnp.zeros_like(r)
        for i in range(k, ROWS):
            column = jnp.where(row == i, inverse[i][k], column)
        upper = upper + column * jnp.broadcast_to(r[k : k + 1, :], r.shape)
        out = out + column * jnp.broadcast_to(e[k : k + 1, :], e.shape)
    return upper, out


def trailing(a_ref, e_ref, upper, out, turned, first, stop):
    shape = upper.shape
    upper_rows = [jnp.broadcast_to(upper[k : k + 1, :], shape) for k in range(ROWS)]
    out_rows = [jnp.broadcast_to(out[k : k + 1, :], shape) for k in range(ROWS)]
    for q in range(first, stop):
        here = slice(q * ROWS, (q + 1) * ROWS)
        a_part = jnp.zeros_like(upper)
        e_part = jnp.zeros_like(out)
        for k in range(ROWS):
            column = jnp.broadcast_to(turned[here, k : k + 1], shape)
            a_part = a_part + column * upper_rows[k]
            e_part = e_part + column * out_rows[k]
        a_ref[here, :] = a_ref[here, :] - a_part
        e_ref[here, :] = e_ref[here, :] - e_part


def invert_lower(a_ref, e_ref):
    n = a_ref.shape[0]
    i = lax.broadcasted_iota(jnp.int32, (n, n), 0)
    k = lax.broadcasted_iota(jnp.int32, (n, n), 1)
    e_ref[...] = jnp.where(i == k, 1.0, 0.0).astype(F32)
    groups = n // ROWS
    if n % 128:
        for p in range(groups):
            here = slice(p * ROWS, (p + 1) * ROWS)
            r = a_ref[here, :]
            rolled = r
            if p:
                rolled = jnp.concatenate([r[:, p * ROWS :], r[:, : p * ROWS]], axis=1)
            upper, out = panel(r, rolled, e_ref[here, :])
            e_ref[here, :] = out
            if p + 1 < groups:
                trailing(a_ref, e_ref, upper, out, upper.T, p + 1, groups)
        return

    def step(p, carry):
        start = pl.multiple_of(p * ROWS, ROWS)
        r = a_ref[pl.ds(start, ROWS), :]
        rolled = pltpu.roll(r, (n - start) % n, 1)
        upper, out = panel(r, rolled, e_ref[pl.ds(start, ROWS), :])
        e_ref[pl.ds(start, ROWS), :] = out
        turned = upper.T
        row = lax.broadcasted_iota(jnp.int32, turned.shape, 0)
        turned = jnp.where(row >= start + ROWS, turned, 0.0)
        trailing(a_ref, e_ref, upper, out, turned, 0, groups)
        return carry

    lax.fori_loop(0, groups, step, 0)


def sweeps(parts, start, turned=(False,) * SWEEPS):
    n, ranks = start.shape
    count = len(parts)

    def kernel(*refs):
        s_ref, o_ref, a_ref, e_ref = refs[count:]
        gram = jnp.concatenate([r[...] for r in refs[:count]], axis=0)
        subspace = s_ref[...]
        for turn in turned:
            product = exact_tn(gram, subspace) if turn else exact_nn(gram, subspace)
            a_ref[...] = exact_tn(product, product)
            invert_lower(a_ref, e_ref)
            subspace = exact_nt(product, e_ref[...])
        o_ref[...] = subspace

    return pl.pallas_call(
        kernel,
        in_specs=[pl.BlockSpec(memory_space=pltpu.VMEM)] * (count + 1),
        out_specs=pl.BlockSpec(memory_space=pltpu.VMEM),
        out_shape=jax.ShapeDtypeStruct((n, ranks), F32),
        scratch_shapes=[pltpu.VMEM((ranks, ranks), F32)] * 2,
        name="sweeps",
    )(*parts, start)


def swap(value, axis, s):
    n = lax.axis_size(axis)
    return lax.ppermute(value, axis, [(i, i ^ s) for i in range(n)])


def block(value, index, size, dim):
    return lax.dynamic_slice_in_dim(value, index * size, size, dim)


def pieces(count, shares):
    runs = []
    start = 0
    total = sum(shares)
    seen = 0
    for share in shares:
        seen += share
        stop = (count * seen) // total
        if stop > start:
            runs.append((start, stop - start))
            start = stop
    return runs


def fold(value, width):
    while 2 * value.shape[1] <= width and value.shape[0] % (2 * ROWS) == 0:
        half = value.shape[0] // 2
        value = jnp.concatenate([value[:half], value[half:]], axis=1)
    return jnp.pad(value, ((0, (-value.shape[0]) % ROWS), (0, width - value.shape[1])))


def unfold(value, rows, columns):
    width = value.shape[1]
    count = 1
    while 2 * count * columns <= width and (rows // count) % (2 * ROWS) == 0:
        count *= 2
    size = rows // count
    parts = [None] * count
    for place in range(count):
        bits = place
        index = 0
        span = count
        step = 1
        while span > 1:
            index += (bits & 1) * (count // (2 * step))
            bits >>= 1
            span //= 2
            step *= 2
        parts[index] = value[:size, place * columns : (place + 1) * columns]
    return jnp.concatenate(parts, axis=0)


def relative_rows(value, place, count):
    size = value.shape[0] // count
    return jnp.concatenate([block(value, place ^ s, size, 0) for s in range(count)], axis=0)


def shards(gradient, start_in, start_out, start_x, start_y):
    f = lax.axis_index("fsdp")
    m = lax.axis_index("mode")
    joint = lax.axis_index(("fsdp", "mode"))
    nf = lax.axis_size("fsdp")
    nm = lax.axis_size("mode")
    nx, ny, nc, no, ni = gradient.shape
    slots = ny * nc
    flat = gradient.reshape(nx, slots, no, ni)
    per_mode = slots // nm
    per_fsdp = slots // nf

    def cut(place, count, per, run, after=None):
        source = flat if after is None else lax.optimization_barrier((flat, after))[0]
        return [
            lax.dynamic_slice(source, (0, (place ^ s) * per + run[0], 0, 0), (nx, run[1], no, ni))
            for s in range(1, count)
        ]

    def exchange(axis, parts):
        return [swap(part, axis, s + 1) for s, part in enumerate(parts)]

    mode_runs = pieces(per_mode, (1, 4, 1, 1, 1))
    fsdp_runs = pieces(per_fsdp, (3, 1))

    def cut_mode(k, after=None):
        return cut(m, nm, per_mode, mode_runs[k], after)

    def cut_fsdp(k, after=None):
        return cut(f, nf, per_fsdp, fsdp_runs[k], after)

    mode_cuts = [cut_mode(0)]
    fsdp_cuts = [cut_fsdp(0, mode_cuts[0][0])]
    for k in range(1, len(fsdp_runs)):
        fsdp_cuts.append(cut_fsdp(k, fsdp_cuts[0][0]))
    for k in range(1, len(mode_runs)):
        mode_cuts.append(cut_mode(k, fsdp_cuts[-1][0]))
    mode_parts = []
    for parts in mode_cuts:
        mode_parts.append(exchange("mode", parts))
    fsdp_parts = []
    for parts in fsdp_cuts:
        fsdp_parts.append(exchange("fsdp", parts))

    source = lax.optimization_barrier((gradient, mode_cuts[1][0]))[0]
    gram_y = gram_y_part(source)
    rows = source.reshape(nx * slots * no, ni)
    gram_in = lax.dot_general(
        rows, rows, (((0,), (0,)), ((), ())), precision=lax.Precision.HIGH
    )
    gram_out = jnp.zeros((nf * no, nf * no), F32)
    for run, parts in zip(fsdp_runs, fsdp_parts):
        gram_out = gram_out_part(flat, f * per_fsdp + run[0], parts, f, gram_out)

    rows_in = ni // nf
    folded_y = fold(gram_y, ni)

    def message(s):
        return jnp.concatenate(
            [block(gram_in, f ^ s, rows_in, 0), fold(block(gram_out, f ^ s, no, 0), ni), folded_y],
            axis=0,
        )

    messages = [message(s) for s in range(nf)]
    summed = messages[0]
    for value in [swap(messages[s], "fsdp", s) for s in range(1, nf)]:
        summed = summed + value
    values = [swap(summed, "mode", s) for s in range(1, nm)]
    for value in values:
        summed = summed + value
    gram_y = unfold(summed[summed.shape[0] - folded_y.shape[0] :], ny, ny)
    summed = summed[: summed.shape[0] - folded_y.shape[0]]
    gathered = [summed] + [swap(summed, "fsdp", s) for s in range(1, nf)]
    full_in = sweeps([g[:rows_in] for g in gathered], start_in, (False, True))
    factor_y = sweeps([gram_y], start_y)
    full_out = sweeps(
        [unfold(g[rows_in:], no, nf * no) for g in gathered],
        relative_rows(start_out, f, nf),
        (True, False),
    )

    projected = jnp.concatenate(
        [
            project(flat, f * per_fsdp + run[0], parts, full_in, full_out)
            for run, parts in zip(fsdp_runs, fsdp_parts)
        ],
        axis=1,
    )
    nb = projected.shape[2] // nf
    by_b = [block(projected, f ^ s, nb, 2) for s in range(nf)]
    by_b = by_b[:1] + [swap(by_b[s], "fsdp", s) for s in range(1, nf)]
    reduced = contract_y(by_b, f, factor_y, nc)
    na = reduced.shape[3]
    reduced = reduced.reshape(nx, -1, na)
    nr = reduced.shape[1] // nm

    gram_x = jnp.zeros((nx * nm, nx * nm), F32)
    for run, parts in zip(mode_runs, mode_parts):
        gram_x = gram_x_part(flat, m * per_mode + run[0], parts, m, gram_x)
    s = 1
    while s < nm:
        gram_x = gram_x + swap(gram_x, "mode", s)
        s *= 2
    s = 1
    while s < nf:
        gram_x = gram_x + swap(gram_x, "fsdp", s)
        s *= 2
    by_x = [block(reduced, m ^ s, nr, 1) for s in range(nm)]
    by_x = by_x[:1] + [swap(by_x[s], "mode", s) for s in range(1, nm)]
    factor_x = sweeps([gram_x], start_x)
    by_p = contract_x(by_x, m, factor_x)
    np_ = by_p.shape[0] // nm
    by_p = [block(by_p, m ^ s, np_, 0) for s in range(nm)]
    by_p = by_p[:1] + [swap(by_p[s], "mode", s) for s in range(1, nm)]
    core = assemble(by_p, m).reshape(np_, nb, -1, nc, na)

    rows_in = ni // (nf * nm)
    factor_in = block(full_in, joint, rows_in, 0)
    return (factor_in, full_out[:no], factor_x, factor_y, core)


def solution(mesh):
    in_specs = (P("mode", None, None, "fsdp", None), P(), P(), P(), P())
    out_specs = (
        P(("fsdp", "mode"), None),
        P("fsdp", None),
        P(),
        P(),
        P("mode", "fsdp", None, None, None),
    )
    return jax.shard_map(shards, mesh=mesh, in_specs=in_specs, out_specs=out_specs, check_vma=False)
```

```python
import jax
import jax.numpy as jnp
from jax import lax
from jax.experimental import pallas as pl
from jax.experimental.pallas import tpu as pltpu
from jax.sharding import PartitionSpec as P

SWEEPS = 2
ROWS = 8

precise = lax.Precision.HIGHEST
F32 = jnp.float32
BF16 = jnp.bfloat16


def split(a):
    high = a.astype(BF16)
    low = (a - high.astype(F32)).astype(BF16)
    return high, low


def dot_nt(a, b):
    return lax.dot_general(a, b, (((1,), (1,)), ((), ())), preferred_element_type=F32)


def dot_nn(a, b):
    return jnp.dot(a, b, preferred_element_type=F32)


def exact_nn(a, b):
    return lax.dot_general(
        a, b, (((1,), (0,)), ((), ())), precision=precise, preferred_element_type=F32
    )


def exact_nt(a, b):
    return lax.dot_general(
        a, b, (((1,), (1,)), ((), ())), precision=precise, preferred_element_type=F32
    )


def exact_tn(a, b):
    return lax.dot_general(
        a, b, (((0,), (0,)), ((), ())), precision=precise, preferred_element_type=F32
    )


def symmetric(acc, n):
    cross = acc[:, n:]
    return acc[:, :n] + cross + cross.T


def rows_gram(a):
    high, low = split(a)
    return dot_nt(high, jnp.concatenate([high, low], axis=0))


def same_row(n):
    r = lax.broadcasted_iota(jnp.int32, (n, n), 0)
    c = lax.broadcasted_iota(jnp.int32, (n, n), 1)
    return (r & (ROWS - 1)) == (c & (ROWS - 1))


def group_select(n, group, place=lambda k: k):
    r = lax.broadcasted_iota(jnp.int32, (n // group, n), 0)
    c = lax.broadcasted_iota(jnp.int32, (n // group, n), 1)
    return jnp.where(r == place(c // group), 1.0, 0.0).astype(F32)


def gram_y_kernel(g_ref, o_ref, acc_ref):
    _, ny, nc, no, ni = g_ref.shape
    n = ny * ROWS

    @pl.when(pl.program_id(0) == 0)
    def _():
        acc_ref[...] = jnp.zeros_like(acc_ref)

    acc_ref[...] += rows_gram(
        jnp.concatenate(
            [
                g_ref[0, :, c, t * ROWS : (t + 1) * ROWS, :].reshape(n, ni)
                for c in range(nc)
                for t in range(no // ROWS)
            ],
            axis=1,
        )
    )

    @pl.when(pl.program_id(0) == pl.num_programs(0) - 1)
    def _():
        full = jnp.where(same_row(n), symmetric(acc_ref[...], n), 0.0)
        select = group_select(n, ROWS)
        o_ref[...] = exact_nt(exact_nn(select, full), select)


def gram_y_part(gradient):
    nx, ny, nc, no, ni = gradient.shape
    return pl.pallas_call(
        gram_y_kernel,
        grid=(nx,),
        in_specs=[pl.BlockSpec((1, ny, nc, no, ni), lambda x: (x, 0, 0, 0, 0))],
        out_specs=pl.BlockSpec((ny, ny), lambda x: (0, 0)),
        out_shape=jax.ShapeDtypeStruct((ny, ny), F32),
        scratch_shapes=[pltpu.VMEM((ny * ROWS, 2 * ny * ROWS), F32)],
        name="gram_y",
    )(gradient)


def gram_parts(kernel_rows, finish, own, base, received, place, prev, n, outs):
    nx, count, no, ni = received[0].shape
    sources = len(received) + 1
    n_prev = 0 if prev is None else 1
    n_out = len(outs)

    def kernel(s_ref, own_ref, *refs):
        parts = (own_ref, *refs[: sources - 1])
        o_refs = refs[sources - 1 + n_prev : sources - 1 + n_prev + n_out]
        acc_ref = refs[sources - 1 + n_prev + n_out]

        @pl.when(pl.program_id(0) == 0)
        def _():
            if n_prev:
                acc_ref[...] = refs[sources - 1][...]
            else:
                acc_ref[...] = jnp.zeros_like(acc_ref)

        kernel_rows(parts, acc_ref)

        @pl.when(pl.program_id(0) == pl.num_programs(0) - 1)
        def _():
            if finish is None:
                o_refs[0][...] = acc_ref[...]
            else:
                finish(acc_ref, s_ref[1], o_refs)

    grid_spec = pltpu.PrefetchScalarGridSpec(
        num_scalar_prefetch=1,
        grid=(count,),
        in_specs=[pl.BlockSpec((nx, 1, no, ni), lambda u, s: (0, s[0] + u, 0, 0))]
        + [pl.BlockSpec((nx, 1, no, ni), lambda u, s: (0, u, 0, 0))] * (sources - 1)
        + [pl.BlockSpec((n, 2 * n), lambda u, s: (0, 0))] * n_prev,
        out_specs=[pl.BlockSpec(o, lambda u, s: (0, 0)) for o in outs],
        scratch_shapes=[pltpu.VMEM((n, 2 * n), F32)],
    )
    scalars = jnp.stack([base, place]).astype(jnp.int32)
    return pl.pallas_call(
        kernel, grid_spec=grid_spec, out_shape=[jax.ShapeDtypeStruct(o, F32) for o in outs]
    )(scalars, own, *received, *(() if prev is None else (prev,)))


def gram_x_part(own, base, received, place, prev, last):
    nx, _, no, ni = received[0].shape
    total = (len(received) + 1) * nx
    n = total * ROWS

    def add(parts, acc_ref):
        pair = 2 if no % (2 * ROWS) == 0 else 1

        def rows(start):
            own_rows = [r[:, 0, pl.ds(start, ROWS), :] for r in parts]
            return jnp.concatenate([r.reshape(nx * ROWS, ni) for r in own_rows], axis=0)

        def step(t, carry):
            starts = [pl.multiple_of((pair * t + j) * ROWS, ROWS) for j in range(pair)]
            acc_ref[...] += rows_gram(jnp.concatenate([rows(k) for k in starts], axis=1))
            return carry

        lax.fori_loop(0, no // (pair * ROWS), step, 0)

    def finish(acc_ref, mine, o_refs):
        full = jnp.where(same_row(n), symmetric(acc_ref[...], n), 0.0)
        select = group_select(n, ROWS, lambda k: ((k // nx) ^ mine) * nx + k % nx)
        o_refs[0][...] = exact_nt(exact_nn(select, full), select)

    outs = [(total, total)] if last else [(n, 2 * n)]
    return gram_parts(add, finish if last else None, own, base, received, place, prev, n, outs)[0]


def gram_out_part(own, base, received, place, prev, last):
    nx, _, no, _ = received[0].shape
    sources = len(received) + 1
    n = sources * no

    def add(parts, acc_ref):
        def step(k, carry):
            pair = [jnp.concatenate([r[2 * k + j, 0] for r in parts], axis=0) for j in range(2)]
            acc_ref[...] += rows_gram(jnp.concatenate(pair, axis=1))
            return carry

        lax.fori_loop(0, nx // 2, step, 0)

    def finish(acc_ref, mine, o_refs):
        r = lax.broadcasted_iota(jnp.int32, (n, n), 0)
        c = lax.broadcasted_iota(jnp.int32, (n, n), 1)
        select = jnp.where(r == ((c // no) ^ mine) * no + c % no, 1.0, 0.0).astype(F32)
        full = exact_nt(symmetric(acc_ref[...], n), select)
        for d in range(sources):
            o_refs[d][...] = full[d * no : (d + 1) * no]

    outs = [(no, n)] * sources if last else [(n, 2 * n)]
    return gram_parts(add, finish if last else None, own, base, received, place, prev, n, outs)


def project(own, base, received, first, slots, factor_in, turned_out, prev):
    nx, count, no, ni = received[0].shape
    sources = len(received) + 1
    ra = factor_in.shape[1]
    nb = turned_out.shape[0] // sources
    n_prev = 0 if prev is None else sources

    def kernel(s_ref, own_ref, *refs):
        parts = (own_ref, *refs[: sources - 1])
        in_ref, out_ref = refs[sources - 1 : sources + 1]
        v_refs = refs[sources + 1 + n_prev :]
        in_high, in_low = split(in_ref[...])
        in_both = jnp.concatenate([in_high, in_low], axis=1)
        out_high, out_low = split(out_ref[...])

        def step(x, carry):
            high, low = split(jnp.concatenate([r[x, 0] for r in parts], axis=0))
            u = dot_nn(high, in_both)
            u = u[:, :ra] + (u[:, ra:] + dot_nn(low, in_high))
            u_high, u_low = split(u)
            v = dot_nn(out_high, jnp.concatenate([u_high, u_low], axis=1))
            v = v[:, :ra] + (v[:, ra:] + dot_nn(out_low, u_high))
            for d in range(sources):
                v_refs[d][x, 0] = v[d * nb : (d + 1) * nb]
            return carry

        lax.fori_loop(0, nx, step, 0)

    grid_spec = pltpu.PrefetchScalarGridSpec(
        num_scalar_prefetch=1,
        grid=(count,),
        in_specs=[pl.BlockSpec((nx, 1, no, ni), lambda u, s: (0, s[0] + u, 0, 0))]
        + [pl.BlockSpec((nx, 1, no, ni), lambda u, s: (0, u, 0, 0))] * (sources - 1)
        + [
            pl.BlockSpec(factor_in.shape, lambda u, s: (0, 0)),
            pl.BlockSpec(turned_out.shape, lambda u, s: (0, 0)),
        ]
        + [pl.BlockSpec(memory_space=pl.ANY)] * n_prev,
        out_specs=[pl.BlockSpec((nx, 1, nb, ra), lambda u, s: (0, first + u, 0, 0))] * sources,
    )
    return pl.pallas_call(
        kernel,
        grid_spec=grid_spec,
        out_shape=[jax.ShapeDtypeStruct((nx, slots, nb, ra), F32)] * sources,
        input_output_aliases={sources + 3 + d: d for d in range(n_prev)},
        name="project",
    )(jnp.stack([base]).astype(jnp.int32), own, *received, factor_in, turned_out, *(prev or ()))


def contract_y(parts, place, factor_y, nc):
    nx, count, nb, na = parts[0].shape
    _, nq = factor_y.shape
    sources = len(parts)
    x_step = 4 if nx % 4 == 0 else nx
    q_step = 2 if nq % 2 == 0 else 1

    def kernel(s_ref, f_ref, *refs):
        o_ref = refs[sources]
        mine = s_ref[0]
        for q0 in range(0, nq, q_step):
            totals = {}
            for r in range(sources):
                for u in range(count):
                    slot = (mine ^ r) * count + u
                    scales = [f_ref[slot // nc, q0 + j] for j in range(q_step)]
                    for x in range(x_step):
                        value = refs[r][x, u]
                        for j in range(q_step):
                            term = scales[j] * value
                            for c in range(nc):
                                if count % nc == 0:
                                    if u % nc != c:
                                        continue
                                    part = term
                                else:
                                    part = jnp.where(slot % nc == c, term, 0.0)
                                key = (j, x, c)
                                totals[key] = totals[key] + part if key in totals else part
            for (j, x, c), total in totals.items():
                o_ref[x, :, (q0 + j) * nc + c, :] = total

    return pl.pallas_call(
        kernel,
        grid=(nx // x_step,),
        in_specs=[
            pl.BlockSpec(memory_space=pltpu.SMEM),
            pl.BlockSpec(memory_space=pltpu.SMEM),
        ]
        + [pl.BlockSpec((x_step, count, nb, na), lambda x: (x, 0, 0, 0))] * sources,
        out_specs=pl.BlockSpec((x_step, nb, nq * nc, na), lambda x: (x, 0, 0, 0)),
        out_shape=jax.ShapeDtypeStruct((nx, nb, nq * nc, na), F32),
        name="contract_y",
    )(jnp.stack([place]).astype(jnp.int32), factor_y, *parts)


def contract_x(parts, place, factor_x):
    nx, rows, na = parts[0].shape
    sources = len(parts)
    np_ = factor_x.shape[1] // sources

    def kernel(s_ref, f_ref, *refs):
        mine = s_ref[0]
        for d in range(sources):
            totals = [None] * np_
            for r in range(sources):
                for x in range(nx):
                    value = refs[r][x]
                    for p in range(np_):
                        scale = f_ref[(mine ^ r) * nx + x, (mine ^ d) * np_ + p]
                        term = scale * value
                        totals[p] = term if totals[p] is None else totals[p] + term
            for p in range(np_):
                refs[sources + d][p] = totals[p]

    return pl.pallas_call(
        kernel,
        in_specs=[
            pl.BlockSpec(memory_space=pltpu.SMEM),
            pl.BlockSpec(memory_space=pltpu.SMEM),
        ]
        + [pl.BlockSpec(memory_space=pltpu.VMEM)] * sources,
        out_specs=[pl.BlockSpec(memory_space=pltpu.VMEM)] * sources,
        out_shape=[jax.ShapeDtypeStruct((np_, rows, na), F32)] * sources,
        name="contract_x",
    )(jnp.stack([place]).astype(jnp.int32), factor_x, *parts)


def assemble(parts, place):
    sources = len(parts)
    np_, rows, na = parts[0].shape

    def kernel(s_ref, *refs):
        for r in range(sources):
            refs[sources][:, s_ref[0] ^ r] = refs[r][...]

    return pl.pallas_call(
        kernel,
        in_specs=[pl.BlockSpec(memory_space=pltpu.SMEM)]
        + [pl.BlockSpec(memory_space=pltpu.VMEM)] * sources,
        out_specs=pl.BlockSpec(memory_space=pltpu.VMEM),
        out_shape=jax.ShapeDtypeStruct((np_, sources, rows, na), F32),
        name="assemble",
    )(jnp.stack([place]).astype(jnp.int32), *parts)


def splat(value, i, k):
    column = jnp.broadcast_to(value[:, k : k + 1], value.shape)
    return jnp.broadcast_to(column[i : i + 1, :], value.shape)


def inverse_factor(d):
    scale = [None] * ROWS
    lower = [[None] * ROWS for _ in range(ROWS)]
    for k in range(ROWS):
        y = lax.rsqrt(d[k][k])
        scale[k] = y * (1.5 - 0.5 * d[k][k] * y * y)
        for i in range(k + 1, ROWS):
            lower[i][k] = d[i][k] * scale[k]
        for j in range(k + 1, ROWS):
            for i in range(j, ROWS):
                d[i][j] = d[i][j] - lower[i][k] * lower[j][k]
    inverse = [[None] * ROWS for _ in range(ROWS)]
    for k in range(ROWS):
        inverse[k][k] = scale[k]
        for i in range(k + 1, ROWS):
            total = lower[i][k] * inverse[k][k]
            for j in range(k + 1, i):
                total = total + lower[i][j] * inverse[j][k]
            inverse[i][k] = -scale[i] * total
    return inverse


def panel(r, rolled, e):
    row = lax.broadcasted_iota(jnp.int32, r.shape, 0)
    d = [[splat(rolled, i, k) if i >= k else None for k in range(ROWS)] for i in range(ROWS)]
    inverse = inverse_factor(d)
    upper = jnp.zeros_like(r)
    out = jnp.zeros_like(e)
    for k in range(ROWS):
        column = jnp.zeros_like(r)
        for i in range(k, ROWS):
            column = jnp.where(row == i, inverse[i][k], column)
        upper = upper + column * jnp.broadcast_to(r[k : k + 1, :], r.shape)
        out = out + column * jnp.broadcast_to(e[k : k + 1, :], e.shape)
    return upper, out


def trailing(a_ref, e_ref, upper, out, turned, first, stop):
    shape = upper.shape
    upper_rows = [jnp.broadcast_to(upper[k : k + 1, :], shape) for k in range(ROWS)]
    out_rows = [jnp.broadcast_to(out[k : k + 1, :], shape) for k in range(ROWS)]
    for q in range(first, stop):
        here = slice(q * ROWS, (q + 1) * ROWS)
        a_part = jnp.zeros_like(upper)
        e_part = jnp.zeros_like(out)
        for k in range(ROWS):
            column = jnp.broadcast_to(turned[here, k : k + 1], shape)
            a_part = a_part + column * upper_rows[k]
            e_part = e_part + column * out_rows[k]
        a_ref[here, :] = a_ref[here, :] - a_part
        e_ref[here, :] = e_ref[here, :] - e_part


def invert_lower(a_ref, e_ref):
    n = a_ref.shape[0]
    i = lax.broadcasted_iota(jnp.int32, (n, n), 0)
    k = lax.broadcasted_iota(jnp.int32, (n, n), 1)
    e_ref[...] = jnp.where(i == k, 1.0, 0.0).astype(F32)
    groups = n // ROWS
    if n % 128:
        for p in range(groups):
            here = slice(p * ROWS, (p + 1) * ROWS)
            r = a_ref[here, :]
            rolled = r
            if p:
                rolled = jnp.concatenate([r[:, p * ROWS :], r[:, : p * ROWS]], axis=1)
            upper, out = panel(r, rolled, e_ref[here, :])
            e_ref[here, :] = out
            if p + 1 < groups:
                trailing(a_ref, e_ref, upper, out, upper.T, p + 1, groups)
        return

    def step(p, carry):
        start = pl.multiple_of(p * ROWS, ROWS)
        r = a_ref[pl.ds(start, ROWS), :]
        rolled = pltpu.roll(r, (n - start) % n, 1)
        upper, out = panel(r, rolled, e_ref[pl.ds(start, ROWS), :])
        e_ref[pl.ds(start, ROWS), :] = out
        turned = upper.T
        row = lax.broadcasted_iota(jnp.int32, turned.shape, 0)
        turned = jnp.where(row >= start + ROWS, turned, 0.0)
        trailing(a_ref, e_ref, upper, out, turned, 0, groups)
        return carry

    lax.fori_loop(0, groups, step, 0)


def sweeps(parts, start, turned=(False,) * SWEEPS, place=None, cuts=1, keep=None):
    n, ranks = start.shape
    count = len(parts)
    size = ranks // cuts
    n_out = 1 if place is None else 2

    def kernel(place_ref, *refs):
        s_ref = refs[count]
        outs = refs[count + 1 : count + 1 + n_out]
        a_ref, e_ref = refs[count + 1 + n_out :]
        gram = jnp.concatenate([r[:keep] for r in refs[:count]], axis=0)
        subspace = s_ref[...]
        for turn in turned:
            product = exact_tn(gram, subspace) if turn else exact_nn(gram, subspace)
            a_ref[...] = exact_tn(product, product)
            invert_lower(a_ref, e_ref)
            subspace = exact_nt(product, e_ref[...])
        outs[0][...] = subspace
        if place is not None:
            mine = place_ref[0]
            r = lax.broadcasted_iota(jnp.int32, (ranks, ranks), 0)
            c = lax.broadcasted_iota(jnp.int32, (ranks, ranks), 1)
            select = jnp.where(c == ((r // size) ^ mine) * size + r % size, 1.0, 0.0).astype(F32)
            outs[1][...] = exact_nt(exact_nn(select, e_ref[...]), product)

    return pl.pallas_call(
        kernel,
        in_specs=[pl.BlockSpec(memory_space=pltpu.SMEM)]
        + [pl.BlockSpec(memory_space=pltpu.VMEM)] * (count + 1),
        out_specs=[pl.BlockSpec(memory_space=pltpu.VMEM)] * n_out,
        out_shape=[jax.ShapeDtypeStruct((n, ranks), F32), jax.ShapeDtypeStruct((ranks, n), F32)][
            :n_out
        ],
        scratch_shapes=[pltpu.VMEM((ranks, ranks), F32)] * 2,
        name="sweeps",
    )(jnp.stack([0 if place is None else place]).astype(jnp.int32), *parts, start)


def swap(value, axis, s):
    n = lax.axis_size(axis)
    return lax.ppermute(value, axis, [(i, i ^ s) for i in range(n)])


def total_over(value, axis):
    n = lax.axis_size(axis)
    base = 1
    while base < n:
        group = min(4, n // base)
        arrived = [swap(value, axis, base * k) for k in range(1, group)]
        for other in arrived:
            value = value + other
        base *= group
    return value


def block(value, index, size, dim):
    return lax.dynamic_slice_in_dim(value, index * size, size, dim)


def pieces(count, shares):
    runs = []
    start = 0
    total = sum(shares)
    seen = 0
    for share in shares:
        seen += share
        stop = (count * seen) // total
        if stop > start:
            runs.append((start, stop - start))
            start = stop
    return runs


def all_but(value, axis):
    return [swap(value, axis, s) for s in range(1, lax.axis_size(axis))]


def added(values):
    total = values[0]
    for value in values[1:]:
        total = total + value
    return total


def relative_rows(value, place, count):
    size = value.shape[0] // count
    return jnp.concatenate([block(value, place ^ s, size, 0) for s in range(count)], axis=0)


def shards(gradient, start_in, start_out, start_x, start_y):
    f = lax.axis_index("fsdp")
    m = lax.axis_index("mode")
    joint = lax.axis_index(("fsdp", "mode"))
    nf = lax.axis_size("fsdp")
    nm = lax.axis_size("mode")
    nx, ny, nc, no, ni = gradient.shape
    slots = ny * nc
    flat = gradient.reshape(nx, slots, no, ni)
    per_mode = slots // nm
    per_fsdp = slots // nf

    def cut(place, count, per, run, after=None):
        source = flat if after is None else lax.optimization_barrier((flat, after))[0]
        return [
            lax.dynamic_slice(source, (0, (place ^ s) * per + run[0], 0, 0), (nx, run[1], no, ni))
            for s in range(1, count)
        ]

    def exchange(axis, parts):
        return [swap(part, axis, s + 1) for s, part in enumerate(parts)]

    mode_runs = pieces(per_mode, (2, 1, 1, 1, 1, 2))
    fsdp_runs = pieces(per_fsdp, (1, 3))

    def cut_mode(k, after=None):
        return cut(m, nm, per_mode, mode_runs[k], after)

    def cut_fsdp(k, after=None):
        return cut(f, nf, per_fsdp, fsdp_runs[k], after)

    mode_cuts = [cut_mode(0)]
    fsdp_cuts = [cut_fsdp(0, mode_cuts[0][0])]
    for k in range(1, len(fsdp_runs)):
        fsdp_cuts.append(cut_fsdp(k, fsdp_cuts[0][0]))
    for k in range(1, len(mode_runs)):
        mode_cuts.append(cut_mode(k, fsdp_cuts[-1][0]))
    mode_parts = []
    for parts in mode_cuts:
        mode_parts.append(exchange("mode", parts))
    fsdp_parts = []
    for parts in fsdp_cuts:
        fsdp_parts.append(exchange("fsdp", parts))

    source = lax.optimization_barrier((gradient, fsdp_cuts[0][0]))[0]
    gram_y = gram_y_part(source)
    groups_y = range(0, ny, ROWS)
    folded_y = jnp.concatenate([gram_y[k : k + ROWS] for k in groups_y], axis=1)
    folded_y = jnp.pad(folded_y, ((0, 0), (0, ni - folded_y.shape[1])))
    rows = source.reshape(nx * slots * no, ni)
    gram_in = lax.dot_general(rows, rows, (((0,), (0,)), ((), ())), precision=lax.Precision.HIGH)

    rows_in = ni // nf
    rows_one = rows_in // nm
    messages = [
        jnp.concatenate([block(gram_in, f ^ s, rows_in, 0), folded_y], axis=0)
        for s in range(nf)
    ]
    arrived = [swap(messages[s], "fsdp", s) for s in range(1, nf)]
    sum_in = added([messages[0]] + arrived)
    messages = [
        jnp.concatenate([block(sum_in, m ^ s, rows_one, 0), sum_in[rows_in:]], axis=0)
        for s in range(nm)
    ]
    arrived = [swap(messages[s], "mode", s) for s in range(1, nm)]
    sum_in = added([messages[0]] + arrived)
    folded_y = sum_in[rows_one:]
    gram_y = jnp.concatenate(
        [folded_y[:, k // ROWS * ny : (k // ROWS + 1) * ny] for k in groups_y], axis=0
    )
    sum_in = sum_in[:rows_one]
    sum_in = jnp.concatenate([sum_in] + all_but(sum_in, "mode"), axis=0)
    gathered = [sum_in] + all_but(sum_in, "fsdp")
    (full_in,) = sweeps(gathered, start_in, (False, True))
    (factor_y,) = sweeps([gram_y], start_y)

    gram_out = [None]
    for k, (run, parts) in enumerate(zip(fsdp_runs, fsdp_parts)):
        last = k == len(fsdp_runs) - 1
        base = f * per_fsdp + run[0]
        gram_out = gram_out_part(flat, base, parts, f, gram_out[0], last)
    sum_out = added([gram_out[0]] + [swap(gram_out[s], "fsdp", s) for s in range(1, nf)])
    sum_out = added([sum_out] + all_but(sum_out, "mode"))
    gathered = [sum_out] + all_but(sum_out, "fsdp")
    full_out, turned_out = sweeps(gathered, relative_rows(start_out, f, nf), (True, False), f, nf)

    by_b = None
    for run, parts in zip(fsdp_runs, fsdp_parts):
        base = f * per_fsdp + run[0]
        by_b = project(flat, base, parts, run[0], per_fsdp, full_in, turned_out, by_b)
    by_b = [by_b[0]] + [swap(by_b[s], "fsdp", s) for s in range(1, nf)]
    reduced = contract_y(by_b, f, factor_y, nc)
    nb, na = reduced.shape[1], reduced.shape[3]
    reduced = reduced.reshape(nx, -1, na)
    nr = reduced.shape[1] // nm

    gram_x = None
    for k, (run, parts) in enumerate(zip(mode_runs, mode_parts)):
        last = k == len(mode_runs) - 1
        gram_x = gram_x_part(flat, m * per_mode + run[0], parts, m, gram_x, last)
    gram_x = total_over(gram_x, "mode")
    gram_x = total_over(gram_x, "fsdp")
    by_x = [block(reduced, m ^ s, nr, 1) for s in range(nm)]
    by_x = by_x[:1] + [swap(by_x[s], "mode", s) for s in range(1, nm)]
    (factor_x,) = sweeps([gram_x], start_x)
    by_p = contract_x(by_x, m, factor_x)
    by_p = [by_p[0]] + [swap(by_p[s], "mode", s) for s in range(1, nm)]
    core = assemble(by_p, m)
    core = core.reshape(core.shape[0], nb, -1, nc, na)

    rows_in = ni // (nf * nm)
    factor_in = block(full_in, joint, rows_in, 0)
    return (factor_in, full_out[:no], factor_x, factor_y, core)


def solution(mesh):
    in_specs = (P("mode", None, None, "fsdp", None), P(), P(), P(), P())
    out_specs = (
        P(("fsdp", "mode"), None),
        P("fsdp", None),
        P(),
        P(),
        P("mode", "fsdp", None, None, None),
    )
    return jax.shard_map(shards, mesh=mesh, in_specs=in_specs, out_specs=out_specs, check_vma=False)
```

```python
import jax
import jax.numpy as jnp
from jax import lax
from jax.experimental import pallas as pl
from jax.experimental.pallas import tpu as pltpu
from jax.sharding import PartitionSpec as P

SWEEPS = 2
ROWS = 8

precise = lax.Precision.HIGHEST
F32 = jnp.float32
BF16 = jnp.bfloat16


LIMITED = pltpu.CompilerParams(vmem_limit_bytes=50 * 2**20)


def split(a):
    high = a.astype(BF16)
    low = (a - high.astype(F32)).astype(BF16)
    return high, low


def dot_nt(a, b):
    return lax.dot_general(a, b, (((1,), (1,)), ((), ())), preferred_element_type=F32)


def dot_nn(a, b):
    return jnp.dot(a, b, preferred_element_type=F32)


def exact_nn(a, b):
    return lax.dot_general(
        a, b, (((1,), (0,)), ((), ())), precision=precise, preferred_element_type=F32
    )


def exact_nt(a, b):
    return lax.dot_general(
        a, b, (((1,), (1,)), ((), ())), precision=precise, preferred_element_type=F32
    )


def exact_tn(a, b):
    return lax.dot_general(
        a, b, (((0,), (0,)), ((), ())), precision=precise, preferred_element_type=F32
    )


def symmetric(acc, n):
    cross = acc[:, n:]
    return acc[:, :n] + cross + cross.T


def rows_gram(a):
    high, low = split(a)
    return dot_nt(high, jnp.concatenate([high, low], axis=0))


def same_row(n):
    r = lax.broadcasted_iota(jnp.int32, (n, n), 0)
    c = lax.broadcasted_iota(jnp.int32, (n, n), 1)
    return (r & (ROWS - 1)) == (c & (ROWS - 1))


def group_select(n, group, place=lambda k: k):
    r = lax.broadcasted_iota(jnp.int32, (n // group, n), 0)
    c = lax.broadcasted_iota(jnp.int32, (n // group, n), 1)
    return jnp.where(r == place(c // group), 1.0, 0.0).astype(F32)


def gram_y_kernel(g_ref, o_ref, acc_ref):
    _, ny, nc, no, ni = g_ref.shape
    n = ny * ROWS

    @pl.when(pl.program_id(0) == 0)
    def _():
        acc_ref[...] = jnp.zeros_like(acc_ref)

    def step(t, carry):
        here = pl.ds(pl.multiple_of(t * ROWS, ROWS), ROWS)
        acc_ref[...] += rows_gram(
            jnp.concatenate([g_ref[0, :, c, here, :].reshape(n, ni) for c in range(nc)], axis=1)
        )
        return carry

    lax.fori_loop(0, no // ROWS, step, 0)

    @pl.when(pl.program_id(0) == pl.num_programs(0) - 1)
    def _():
        full = jnp.where(same_row(n), symmetric(acc_ref[...], n), 0.0)
        select = group_select(n, ROWS)
        o_ref[...] = exact_nt(exact_nn(select, full), select)


def gram_y_part(gradient):
    nx, ny, nc, no, ni = gradient.shape
    return pl.pallas_call(
        gram_y_kernel,
        grid=(nx,),
        in_specs=[pl.BlockSpec((1, ny, nc, no, ni), lambda x: (x, 0, 0, 0, 0))],
        out_specs=pl.BlockSpec((ny, ny), lambda x: (0, 0)),
        out_shape=jax.ShapeDtypeStruct((ny, ny), F32),
        scratch_shapes=[pltpu.VMEM((ny * ROWS, 2 * ny * ROWS), F32)],
        compiler_params=LIMITED,
        name="gram_y",
    )(gradient)


def gram_parts(kernel_rows, finish, own, base, received, place, prev, n, outs, extra=(), resident=False):
    nx, count, no, ni = received[0].shape
    sources = len(received) + 1
    if resident:
        received = [pltpu.with_memory_space_constraint(part, pltpu.VMEM) for part in received]
        arrived_spec = pl.BlockSpec(memory_space=pltpu.VMEM)
    else:
        arrived_spec = pl.BlockSpec((nx, 1, no, ni), lambda u, s: (0, u, 0, 0))
    n_prev = 0 if prev is None else 1
    n_extra = len(extra)
    first_out = sources - 1 + n_prev + n_extra
    n_out = len(outs)

    def kernel(s_ref, own_ref, *refs):
        parts = refs[: sources - 1]
        if resident:
            parts = [part.at[:, pl.ds(pl.program_id(0), 1)] for part in parts]
        parts = (own_ref, *parts)
        e_refs = refs[first_out - n_extra : first_out]
        o_refs = refs[first_out : first_out + n_out]
        acc_ref = refs[first_out + n_out]

        @pl.when(pl.program_id(0) == 0)
        def _():
            if n_prev:
                acc_ref[...] = refs[sources - 1][...]
            else:
                acc_ref[...] = jnp.zeros_like(acc_ref)

        kernel_rows(parts, acc_ref)

        @pl.when(pl.program_id(0) == pl.num_programs(0) - 1)
        def _():
            if finish is None:
                o_refs[0][...] = acc_ref[...]
            else:
                finish(acc_ref, s_ref[1], o_refs, *e_refs)

    grid_spec = pltpu.PrefetchScalarGridSpec(
        num_scalar_prefetch=1,
        grid=(count,),
        in_specs=[pl.BlockSpec((nx, 1, no, ni), lambda u, s: (0, s[0] + u, 0, 0))]
        + [arrived_spec] * (sources - 1)
        + [pl.BlockSpec((n, 2 * n), lambda u, s: (0, 0))] * n_prev
        + [pl.BlockSpec(e.shape, lambda u, s: (0, 0)) for e in extra],
        out_specs=[pl.BlockSpec(o, lambda u, s: (0, 0)) for o in outs],
        scratch_shapes=[pltpu.VMEM((n, 2 * n), F32)],
    )
    scalars = jnp.stack([base, place]).astype(jnp.int32)
    return pl.pallas_call(
        kernel,
        grid_spec=grid_spec,
        out_shape=[jax.ShapeDtypeStruct(o, F32) for o in outs],
        compiler_params=LIMITED,
    )(scalars, own, *received, *(() if prev is None else (prev,)), *extra)


def gram_x_part(own, base, received, place, prev, last):
    nx, _, no, ni = received[0].shape
    total = (len(received) + 1) * nx
    n = total * ROWS

    def add(parts, acc_ref):
        pair = 2 if no % (2 * ROWS) == 0 else 1

        def rows(start):
            own_rows = [r[:, 0, pl.ds(start, ROWS), :] for r in parts]
            return jnp.concatenate([r.reshape(nx * ROWS, ni) for r in own_rows], axis=0)

        def step(t, carry):
            starts = [pl.multiple_of((pair * t + j) * ROWS, ROWS) for j in range(pair)]
            acc_ref[...] += rows_gram(jnp.concatenate([rows(k) for k in starts], axis=1))
            return carry

        lax.fori_loop(0, no // (pair * ROWS), step, 0)

    def finish(acc_ref, mine, o_refs):
        full = jnp.where(same_row(n), symmetric(acc_ref[...], n), 0.0)
        select = group_select(n, ROWS, lambda k: ((k // nx) ^ mine) * nx + k % nx)
        o_refs[0][...] = exact_nt(exact_nn(select, full), select)

    outs = [(total, total)] if last else [(n, 2 * n)]
    return gram_parts(
        add, finish if last else None, own, base, received, place, prev, n, outs, resident=last
    )[0]


def gram_out_part(own, base, received, place, prev, last, extra):
    nx, _, no, _ = received[0].shape
    sources = len(received) + 1
    n = sources * no

    def add(parts, acc_ref):
        def step(k, carry):
            pair = [jnp.concatenate([r[2 * k + j, 0] for r in parts], axis=0) for j in range(2)]
            acc_ref[...] += rows_gram(jnp.concatenate(pair, axis=1))
            return carry

        lax.fori_loop(0, nx // 2, step, 0)

    def finish(acc_ref, mine, o_refs, e_ref):
        r = lax.broadcasted_iota(jnp.int32, (n, n), 0)
        c = lax.broadcasted_iota(jnp.int32, (n, n), 1)
        select = jnp.where(r == ((c // no) ^ mine) * no + c % no, 1.0, 0.0).astype(F32)
        full = exact_nt(symmetric(acc_ref[...], n), select)
        for d in range(sources):
            o_refs[d][:no] = full[d * no : (d + 1) * no]
            o_refs[d][no:] = e_ref[...]

    outs = [(no + extra.shape[0], n)] * sources if last else [(n, 2 * n)]
    finish, extra = (finish, (extra,)) if last else (None, ())
    return gram_parts(add, finish, own, base, received, place, prev, n, outs, extra)


def project(own, base, received, first, slots, factor_in, turned_out, prev):
    nx, count, no, ni = received[0].shape
    sources = len(received) + 1
    ra = factor_in.shape[1]
    nb = turned_out.shape[0] // sources
    n_prev = 0 if prev is None else sources

    def kernel(s_ref, own_ref, *refs):
        parts = (own_ref, *refs[: sources - 1])
        in_ref, out_ref = refs[sources - 1 : sources + 1]
        v_refs = refs[sources + 1 + n_prev :]
        in_high, in_low = split(in_ref[...])
        in_both = jnp.concatenate([in_high, in_low], axis=1)
        out_high, out_low = split(out_ref[...])

        def step(x, carry):
            high, low = split(jnp.concatenate([r[x, 0] for r in parts], axis=0))
            u = dot_nn(high, in_both)
            u = u[:, :ra] + (u[:, ra:] + dot_nn(low, in_high))
            u_high, u_low = split(u)
            v = dot_nn(out_high, jnp.concatenate([u_high, u_low], axis=1))
            v = v[:, :ra] + (v[:, ra:] + dot_nn(out_low, u_high))
            for d in range(sources):
                v_refs[d][x, 0] = v[d * nb : (d + 1) * nb]
            return carry

        lax.fori_loop(0, nx, step, 0)

    grid_spec = pltpu.PrefetchScalarGridSpec(
        num_scalar_prefetch=1,
        grid=(count,),
        in_specs=[pl.BlockSpec((nx, 1, no, ni), lambda u, s: (0, s[0] + u, 0, 0))]
        + [pl.BlockSpec((nx, 1, no, ni), lambda u, s: (0, u, 0, 0))] * (sources - 1)
        + [
            pl.BlockSpec(factor_in.shape, lambda u, s: (0, 0)),
            pl.BlockSpec(turned_out.shape, lambda u, s: (0, 0)),
        ]
        + [pl.BlockSpec(memory_space=pl.ANY)] * n_prev,
        out_specs=[pl.BlockSpec((nx, 1, nb, ra), lambda u, s: (0, first + u, 0, 0))] * sources,
    )
    return pl.pallas_call(
        kernel,
        grid_spec=grid_spec,
        out_shape=[jax.ShapeDtypeStruct((nx, slots, nb, ra), F32)] * sources,
        input_output_aliases={sources + 3 + d: d for d in range(n_prev)},
        compiler_params=LIMITED,
        name="project",
    )(jnp.stack([base]).astype(jnp.int32), own, *received, factor_in, turned_out, *(prev or ()))


def contract_y(parts, place, factor_y, nc):
    nx, count, nb, na = parts[0].shape
    _, nq = factor_y.shape
    sources = len(parts)
    x_step = 4 if nx % 4 == 0 else nx
    q_step = 2 if nq % 2 == 0 else 1

    def kernel(s_ref, f_ref, *refs):
        o_ref = refs[sources]
        mine = s_ref[0]
        for q0 in range(0, nq, q_step):
            totals = {}
            for r in range(sources):
                for u in range(count):
                    slot = (mine ^ r) * count + u
                    scales = [f_ref[slot // nc, q0 + j] for j in range(q_step)]
                    for x in range(x_step):
                        value = refs[r][x, u]
                        for j in range(q_step):
                            term = scales[j] * value
                            for c in range(nc):
                                if count % nc == 0:
                                    if u % nc != c:
                                        continue
                                    part = term
                                else:
                                    part = jnp.where(slot % nc == c, term, 0.0)
                                key = (j, x, c)
                                totals[key] = totals[key] + part if key in totals else part
            for (j, x, c), total in totals.items():
                o_ref[x, :, (q0 + j) * nc + c, :] = total

    return pl.pallas_call(
        kernel,
        grid=(nx // x_step,),
        in_specs=[
            pl.BlockSpec(memory_space=pltpu.SMEM),
            pl.BlockSpec(memory_space=pltpu.SMEM),
        ]
        + [pl.BlockSpec((x_step, count, nb, na), lambda x: (x, 0, 0, 0))] * sources,
        out_specs=pl.BlockSpec((x_step, nb, nq * nc, na), lambda x: (x, 0, 0, 0)),
        out_shape=jax.ShapeDtypeStruct((nx, nb, nq * nc, na), F32),
        compiler_params=LIMITED,
        name="contract_y",
    )(jnp.stack([place]).astype(jnp.int32), factor_y, *parts)


def contract_x(parts, place, factor_x):
    nx, rows, na = parts[0].shape
    sources = len(parts)
    parts = [pltpu.with_memory_space_constraint(part, pltpu.VMEM) for part in parts]
    np_ = factor_x.shape[1] // sources

    def kernel(s_ref, f_ref, *refs):
        mine = s_ref[0]
        for d in range(sources):
            totals = [None] * np_
            for r in range(sources):
                for x in range(nx):
                    value = refs[r][x]
                    for p in range(np_):
                        scale = f_ref[(mine ^ r) * nx + x, (mine ^ d) * np_ + p]
                        term = scale * value
                        totals[p] = term if totals[p] is None else totals[p] + term
            for p in range(np_):
                refs[sources + d][p] = totals[p]

    return pl.pallas_call(
        kernel,
        in_specs=[
            pl.BlockSpec(memory_space=pltpu.SMEM),
            pl.BlockSpec(memory_space=pltpu.SMEM),
        ]
        + [pl.BlockSpec(memory_space=pltpu.VMEM)] * sources,
        out_specs=[pl.BlockSpec(memory_space=pltpu.VMEM)] * sources,
        out_shape=[jax.ShapeDtypeStruct((np_, rows, na), F32)] * sources,
        compiler_params=LIMITED,
        name="contract_x",
    )(jnp.stack([place]).astype(jnp.int32), factor_x, *parts)


def assemble(parts, place):
    parts = [pltpu.with_memory_space_constraint(part, pltpu.VMEM) for part in parts]
    sources = len(parts)
    np_, rows, na = parts[0].shape

    def kernel(s_ref, *refs):
        for r in range(sources):
            refs[sources][:, s_ref[0] ^ r] = refs[r][...]

    return pl.pallas_call(
        kernel,
        in_specs=[pl.BlockSpec(memory_space=pltpu.SMEM)]
        + [pl.BlockSpec(memory_space=pltpu.VMEM)] * sources,
        out_specs=pl.BlockSpec(memory_space=pltpu.VMEM),
        out_shape=jax.ShapeDtypeStruct((np_, sources, rows, na), F32),
        compiler_params=LIMITED,
        name="assemble",
    )(jnp.stack([place]).astype(jnp.int32), *parts)


def splat(value, i, k):
    column = jnp.broadcast_to(value[:, k : k + 1], value.shape)
    return jnp.broadcast_to(column[i : i + 1, :], value.shape)


def inverse_factor(d):
    scale = [None] * ROWS
    lower = [[None] * ROWS for _ in range(ROWS)]
    for k in range(ROWS):
        y = lax.rsqrt(d[k][k])
        scale[k] = y * (1.5 - 0.5 * d[k][k] * y * y)
        for i in range(k + 1, ROWS):
            lower[i][k] = d[i][k] * scale[k]
        for j in range(k + 1, ROWS):
            for i in range(j, ROWS):
                d[i][j] = d[i][j] - lower[i][k] * lower[j][k]
    inverse = [[None] * ROWS for _ in range(ROWS)]
    for k in range(ROWS):
        inverse[k][k] = scale[k]
        for i in range(k + 1, ROWS):
            total = lower[i][k] * inverse[k][k]
            for j in range(k + 1, i):
                total = total + lower[i][j] * inverse[j][k]
            inverse[i][k] = -scale[i] * total
    return inverse


def panel(r, rolled, e):
    row = lax.broadcasted_iota(jnp.int32, r.shape, 0)
    d = [[splat(rolled, i, k) if i >= k else None for k in range(ROWS)] for i in range(ROWS)]
    inverse = inverse_factor(d)
    upper = jnp.zeros_like(r)
    out = jnp.zeros_like(e)
    for k in range(ROWS):
        column = jnp.zeros_like(r)
        for i in range(k, ROWS):
            column = jnp.where(row == i, inverse[i][k], column)
        upper = upper + column * jnp.broadcast_to(r[k : k + 1, :], r.shape)
        out = out + column * jnp.broadcast_to(e[k : k + 1, :], e.shape)
    return upper, out


def trailing(a_ref, e_ref, upper, out, turned, first, stop):
    shape = upper.shape
    upper_rows = [jnp.broadcast_to(upper[k : k + 1, :], shape) for k in range(ROWS)]
    out_rows = [jnp.broadcast_to(out[k : k + 1, :], shape) for k in range(ROWS)]
    for q in range(first, stop):
        here = slice(q * ROWS, (q + 1) * ROWS)
        a_part = jnp.zeros_like(upper)
        e_part = jnp.zeros_like(out)
        for k in range(ROWS):
            column = jnp.broadcast_to(turned[here, k : k + 1], shape)
            a_part = a_part + column * upper_rows[k]
            e_part = e_part + column * out_rows[k]
        a_ref[here, :] = a_ref[here, :] - a_part
        e_ref[here, :] = e_ref[here, :] - e_part


def invert_lower(a_ref, e_ref):
    n = a_ref.shape[0]
    i = lax.broadcasted_iota(jnp.int32, (n, n), 0)
    k = lax.broadcasted_iota(jnp.int32, (n, n), 1)
    e_ref[...] = jnp.where(i == k, 1.0, 0.0).astype(F32)
    groups = n // ROWS
    if n % 128:
        for p in range(groups):
            here = slice(p * ROWS, (p + 1) * ROWS)
            r = a_ref[here, :]
            rolled = r
            if p:
                rolled = jnp.concatenate([r[:, p * ROWS :], r[:, : p * ROWS]], axis=1)
            upper, out = panel(r, rolled, e_ref[here, :])
            e_ref[here, :] = out
            if p + 1 < groups:
                trailing(a_ref, e_ref, upper, out, upper.T, p + 1, groups)
        return

    def step(p, carry):
        start = pl.multiple_of(p * ROWS, ROWS)
        r = a_ref[pl.ds(start, ROWS), :]
        rolled = pltpu.roll(r, (n - start) % n, 1)
        upper, out = panel(r, rolled, e_ref[pl.ds(start, ROWS), :])
        e_ref[pl.ds(start, ROWS), :] = out
        turned = upper.T
        row = lax.broadcasted_iota(jnp.int32, turned.shape, 0)
        turned = jnp.where(row >= start + ROWS, turned, 0.0)
        trailing(a_ref, e_ref, upper, out, turned, 0, groups)
        return carry

    lax.fori_loop(0, groups, step, 0)


def sweeps(parts, start, turned=(False,) * SWEEPS, place=None, cuts=1, keep=None):
    n, ranks = start.shape
    count = len(parts)
    size = ranks // cuts
    n_out = 1 if place is None else 2

    def kernel(place_ref, *refs):
        s_ref = refs[count]
        outs = refs[count + 1 : count + 1 + n_out]
        a_ref, e_ref = refs[count + 1 + n_out :]
        gram = jnp.concatenate([r[:keep] for r in refs[:count]], axis=0)
        subspace = s_ref[...]
        for turn in turned:
            product = exact_tn(gram, subspace) if turn else exact_nn(gram, subspace)
            a_ref[...] = exact_tn(product, product)
            invert_lower(a_ref, e_ref)
            subspace = exact_nt(product, e_ref[...])
        outs[0][...] = subspace
        if place is not None:
            mine = place_ref[0]
            r = lax.broadcasted_iota(jnp.int32, (ranks, ranks), 0)
            c = lax.broadcasted_iota(jnp.int32, (ranks, ranks), 1)
            select = jnp.where(c == ((r // size) ^ mine) * size + r % size, 1.0, 0.0).astype(F32)
            outs[1][...] = exact_nt(exact_nn(select, e_ref[...]), product)

    return pl.pallas_call(
        kernel,
        in_specs=[pl.BlockSpec(memory_space=pltpu.SMEM)]
        + [pl.BlockSpec(memory_space=pltpu.VMEM)] * (count + 1),
        out_specs=[pl.BlockSpec(memory_space=pltpu.VMEM)] * n_out,
        out_shape=[jax.ShapeDtypeStruct((n, ranks), F32), jax.ShapeDtypeStruct((ranks, n), F32)][
            :n_out
        ],
        scratch_shapes=[pltpu.VMEM((ranks, ranks), F32)] * 2,
        compiler_params=LIMITED,
        name="sweeps",
    )(jnp.stack([0 if place is None else place]).astype(jnp.int32), *parts, start)


def swap(value, axis, s):
    n = lax.axis_size(axis)
    return lax.ppermute(value, axis, [(i, i ^ s) for i in range(n)])


def total_over(value, axis):
    n = lax.axis_size(axis)
    base = 1
    while base < n:
        group = min(4, n // base)
        arrived = [swap(value, axis, base * k) for k in range(1, group)]
        for other in arrived:
            value = value + other
        base *= group
    return value


def block(value, index, size, dim):
    return lax.dynamic_slice_in_dim(value, index * size, size, dim)


def pieces(count, shares):
    runs = []
    start = 0
    total = sum(shares)
    seen = 0
    for share in shares:
        seen += share
        stop = (count * seen) // total
        if stop > start:
            runs.append((start, stop - start))
            start = stop
    return runs


def all_but(value, axis):
    return [swap(value, axis, s) for s in range(1, lax.axis_size(axis))]


def added(values):
    total = values[0]
    for value in values[1:]:
        total = total + value
    return total


def relative_rows(value, place, count):
    size = value.shape[0] // count
    return jnp.concatenate([block(value, place ^ s, size, 0) for s in range(count)], axis=0)


def shards(gradient, start_in, start_out, start_x, start_y):
    f = lax.axis_index("fsdp")
    m = lax.axis_index("mode")
    joint = lax.axis_index(("fsdp", "mode"))
    nf = lax.axis_size("fsdp")
    nm = lax.axis_size("mode")
    nx, ny, nc, no, ni = gradient.shape
    slots = ny * nc
    flat = gradient.reshape(nx, slots, no, ni)
    per_mode = slots // nm
    per_fsdp = slots // nf

    def cut(place, count, per, run, after=None):
        source = flat if after is None else lax.optimization_barrier((flat, after))[0]
        return [
            lax.dynamic_slice(source, (0, (place ^ s) * per + run[0], 0, 0), (nx, run[1], no, ni))
            for s in range(1, count)
        ]

    def exchange(axis, parts):
        return [swap(part, axis, s + 1) for s, part in enumerate(parts)]

    mode_runs = pieces(per_mode, (2, 1, 1, 1, 1, 2))
    fsdp_runs = pieces(per_fsdp, (1, 3))

    def cut_mode(k, after=None):
        return cut(m, nm, per_mode, mode_runs[k], after)

    def cut_fsdp(k, after=None):
        return cut(f, nf, per_fsdp, fsdp_runs[k], after)

    mode_cuts = [cut_mode(0)]
    fsdp_cuts = [cut_fsdp(0, mode_cuts[0][0])]
    for k in range(1, len(fsdp_runs)):
        fsdp_cuts.append(cut_fsdp(k, fsdp_cuts[0][0]))
    for k in range(1, len(mode_runs)):
        mode_cuts.append(cut_mode(k, fsdp_cuts[-1][0]))
    mode_parts = []
    for parts in mode_cuts:
        mode_parts.append(exchange("mode", parts))
    fsdp_parts = []
    for parts in fsdp_cuts:
        fsdp_parts.append(exchange("fsdp", parts))

    source = lax.optimization_barrier((gradient, fsdp_cuts[0][0]))[0]
    gram_y = gram_y_part(source)
    groups_y = range(0, ny, ROWS)
    folded_y = jnp.concatenate([gram_y[k : k + ROWS] for k in groups_y], axis=1)
    folded_y = jnp.pad(folded_y, ((0, 0), (0, nf * no - folded_y.shape[1])))
    rows = source.reshape(nx * slots * no, ni)
    gram_in = lax.dot_general(rows, rows, (((0,), (0,)), ((), ())), precision=lax.Precision.HIGH)

    rows_in = ni // nf
    messages = [block(gram_in, f ^ s, rows_in, 0) for s in range(nf)]
    arrived = [swap(messages[s], "fsdp", s) for s in range(1, nf)]
    sum_in = added([messages[0]] + arrived)
    kept, sent = (block(sum_in, (m & 1) ^ s, rows_in // 2, 0) for s in range(2))
    sum_in = kept + swap(sent, "mode", 1)
    s = 2
    while s < nm:
        sum_in = sum_in + swap(sum_in, "mode", s)
        s *= 2
    sum_in = jnp.concatenate([sum_in, swap(sum_in, "mode", 1)], axis=0)
    gathered = [sum_in] + all_but(sum_in, "fsdp")
    (full_in,) = sweeps(gathered, start_in, (False, True))

    gram_out = [None]
    for k, (run, parts) in enumerate(zip(fsdp_runs, fsdp_parts)):
        last = k == len(fsdp_runs) - 1
        base = f * per_fsdp + run[0]
        gram_out = gram_out_part(flat, base, parts, f, gram_out[0], last, folded_y)
    sum_out = added([gram_out[0]] + [swap(gram_out[s], "fsdp", s) for s in range(1, nf)])
    sum_out = added([sum_out] + all_but(sum_out, "mode"))
    folded_y = sum_out[no:]
    gram_y = jnp.concatenate(
        [folded_y[:, k // ROWS * ny : (k // ROWS + 1) * ny] for k in groups_y], axis=0
    )
    (factor_y,) = sweeps([gram_y], start_y)
    sum_out = sum_out[:no]
    gathered = [sum_out] + all_but(sum_out, "fsdp")
    full_out, turned_out = sweeps(gathered, relative_rows(start_out, f, nf), (True, False), f, nf)

    by_b = None
    for run, parts in zip(fsdp_runs, fsdp_parts):
        base = f * per_fsdp + run[0]
        by_b = project(flat, base, parts, run[0], per_fsdp, full_in, turned_out, by_b)
    by_b = [by_b[0]] + [swap(by_b[s], "fsdp", s) for s in range(1, nf)]
    reduced = contract_y(by_b, f, factor_y, nc)
    nb, na = reduced.shape[1], reduced.shape[3]
    reduced = reduced.reshape(nx, -1, na)
    nr = reduced.shape[1] // nm

    gram_x = None
    for k, (run, parts) in enumerate(zip(mode_runs, mode_parts)):
        last = k == len(mode_runs) - 1
        gram_x = gram_x_part(flat, m * per_mode + run[0], parts, m, gram_x, last)
    gram_x = total_over(gram_x, "mode")
    gram_x = total_over(gram_x, "fsdp")
    by_x = [block(reduced, m ^ s, nr, 1) for s in range(nm)]
    by_x = by_x[:1] + [swap(by_x[s], "mode", s) for s in range(1, nm)]
    (factor_x,) = sweeps([gram_x], start_x)
    by_p = contract_x(by_x, m, factor_x)
    by_p = [by_p[0]] + [swap(by_p[s], "mode", s) for s in range(1, nm)]
    core = assemble(by_p, m)
    core = core.reshape(core.shape[0], nb, -1, nc, na)

    rows_in = ni // (nf * nm)
    factor_in = block(full_in, joint, rows_in, 0)
    return (factor_in, full_out[:no], factor_x, factor_y, core)


def solution(mesh):
    in_specs = (P("mode", None, None, "fsdp", None), P(), P(), P(), P())
    out_specs = (
        P(("fsdp", "mode"), None),
        P("fsdp", None),
        P(),
        P(),
        P("mode", "fsdp", None, None, None),
    )
    return jax.shard_map(shards, mesh=mesh, in_specs=in_specs, out_specs=out_specs, check_vma=False)
```

```python
import jax
import jax.numpy as jnp
from jax import lax
from jax.experimental import pallas as pl
from jax.experimental.pallas import tpu as pltpu
from jax.sharding import PartitionSpec as P

SWEEPS = 2
ROWS = 8

precise = lax.Precision.HIGHEST
F32 = jnp.float32
BF16 = jnp.bfloat16


LIMITED = pltpu.CompilerParams(vmem_limit_bytes=50 * 2**20)


def split(a):
    high = a.astype(BF16)
    low = (a - high.astype(F32)).astype(BF16)
    return high, low


def dot_nt(a, b):
    return lax.dot_general(a, b, (((1,), (1,)), ((), ())), preferred_element_type=F32)


def dot_nn(a, b):
    return jnp.dot(a, b, preferred_element_type=F32)


def exact_nn(a, b):
    return lax.dot_general(
        a, b, (((1,), (0,)), ((), ())), precision=precise, preferred_element_type=F32
    )


def exact_nt(a, b):
    return lax.dot_general(
        a, b, (((1,), (1,)), ((), ())), precision=precise, preferred_element_type=F32
    )


def exact_tn(a, b):
    return lax.dot_general(
        a, b, (((0,), (0,)), ((), ())), precision=precise, preferred_element_type=F32
    )


def symmetric(acc, n):
    cross = acc[:, n:]
    return acc[:, :n] + cross + cross.T


def rows_gram(a):
    high, low = split(a)
    return dot_nt(high, jnp.concatenate([high, low], axis=0))


def same_row(n):
    r = lax.broadcasted_iota(jnp.int32, (n, n), 0)
    c = lax.broadcasted_iota(jnp.int32, (n, n), 1)
    return (r & (ROWS - 1)) == (c & (ROWS - 1))


def group_select(n, group, place=lambda k: k):
    r = lax.broadcasted_iota(jnp.int32, (n // group, n), 0)
    c = lax.broadcasted_iota(jnp.int32, (n // group, n), 1)
    return jnp.where(r == place(c // group), 1.0, 0.0).astype(F32)


def gram_y_kernel(g_ref, o_ref, acc_ref):
    _, ny, nc, no, ni = g_ref.shape
    n = ny * ROWS

    @pl.when(pl.program_id(0) == 0)
    def _():
        acc_ref[...] = jnp.zeros_like(acc_ref)

    def step(t, carry):
        here = pl.ds(pl.multiple_of(t * ROWS, ROWS), ROWS)
        acc_ref[...] += rows_gram(
            jnp.concatenate([g_ref[0, :, c, here, :].reshape(n, ni) for c in range(nc)], axis=1)
        )
        return carry

    lax.fori_loop(0, no // ROWS, step, 0)

    @pl.when(pl.program_id(0) == pl.num_programs(0) - 1)
    def _():
        full = jnp.where(same_row(n), symmetric(acc_ref[...], n), 0.0)
        select = group_select(n, ROWS)
        o_ref[...] = exact_nt(exact_nn(select, full), select)


def gram_y_part(gradient):
    nx, ny, nc, no, ni = gradient.shape
    return pl.pallas_call(
        gram_y_kernel,
        grid=(nx,),
        in_specs=[pl.BlockSpec((1, ny, nc, no, ni), lambda x: (x, 0, 0, 0, 0))],
        out_specs=pl.BlockSpec((ny, ny), lambda x: (0, 0)),
        out_shape=jax.ShapeDtypeStruct((ny, ny), F32),
        scratch_shapes=[pltpu.VMEM((ny * ROWS, 2 * ny * ROWS), F32)],
        compiler_params=LIMITED,
        name="gram_y",
    )(gradient)


def gram_parts(kernel_rows, finish, own, base, received, place, prev, n, outs, extra=(), resident=False):
    nx, count, no, ni = received[0].shape
    sources = len(received) + 1
    if resident:
        received = [pltpu.with_memory_space_constraint(part, pltpu.VMEM) for part in received]
        arrived_spec = pl.BlockSpec(memory_space=pltpu.VMEM)
    else:
        arrived_spec = pl.BlockSpec((nx, 1, no, ni), lambda u, s: (0, u, 0, 0))
    n_prev = 0 if prev is None else 1
    n_extra = len(extra)
    first_out = sources - 1 + n_prev + n_extra
    n_out = len(outs)

    def kernel(s_ref, own_ref, *refs):
        parts = refs[: sources - 1]
        if resident:
            parts = [part.at[:, pl.ds(pl.program_id(0), 1)] for part in parts]
        parts = (own_ref, *parts)
        e_refs = refs[first_out - n_extra : first_out]
        o_refs = refs[first_out : first_out + n_out]
        acc_ref = refs[first_out + n_out]

        @pl.when(pl.program_id(0) == 0)
        def _():
            if n_prev:
                acc_ref[...] = refs[sources - 1][...]
            else:
                acc_ref[...] = jnp.zeros_like(acc_ref)

        kernel_rows(parts, acc_ref)

        @pl.when(pl.program_id(0) == pl.num_programs(0) - 1)
        def _():
            if finish is None:
                o_refs[0][...] = acc_ref[...]
            else:
                finish(acc_ref, s_ref[1], o_refs, *e_refs)

    grid_spec = pltpu.PrefetchScalarGridSpec(
        num_scalar_prefetch=1,
        grid=(count,),
        in_specs=[pl.BlockSpec((nx, 1, no, ni), lambda u, s: (0, s[0] + u, 0, 0))]
        + [arrived_spec] * (sources - 1)
        + [pl.BlockSpec((n, 2 * n), lambda u, s: (0, 0))] * n_prev
        + [pl.BlockSpec(e.shape, lambda u, s: (0, 0)) for e in extra],
        out_specs=[pl.BlockSpec(o, lambda u, s: (0, 0)) for o in outs],
        scratch_shapes=[pltpu.VMEM((n, 2 * n), F32)],
    )
    scalars = jnp.stack([base, place]).astype(jnp.int32)
    return pl.pallas_call(
        kernel,
        grid_spec=grid_spec,
        out_shape=[jax.ShapeDtypeStruct(o, F32) for o in outs],
        compiler_params=LIMITED,
    )(scalars, own, *received, *(() if prev is None else (prev,)), *extra)


def gram_x_part(own, base, received, place, prev, last):
    nx, _, no, ni = received[0].shape
    total = (len(received) + 1) * nx
    n = total * ROWS

    def add(parts, acc_ref):
        pair = 2 if no % (2 * ROWS) == 0 else 1

        def rows(start):
            own_rows = [r[:, 0, pl.ds(start, ROWS), :] for r in parts]
            return jnp.concatenate([r.reshape(nx * ROWS, ni) for r in own_rows], axis=0)

        def step(t, carry):
            starts = [pl.multiple_of((pair * t + j) * ROWS, ROWS) for j in range(pair)]
            acc_ref[...] += rows_gram(jnp.concatenate([rows(k) for k in starts], axis=1))
            return carry

        lax.fori_loop(0, no // (pair * ROWS), step, 0)

    def finish(acc_ref, mine, o_refs):
        full = jnp.where(same_row(n), symmetric(acc_ref[...], n), 0.0)
        select = group_select(n, ROWS, lambda k: ((k // nx) ^ mine) * nx + k % nx)
        o_refs[0][...] = exact_nt(exact_nn(select, full), select)

    outs = [(total, total)] if last else [(n, 2 * n)]
    return gram_parts(
        add, finish if last else None, own, base, received, place, prev, n, outs, resident=last
    )[0]


def gram_out_part(own, base, received, place, prev, last, extra):
    nx, _, no, _ = received[0].shape
    sources = len(received) + 1
    n = sources * no

    def add(parts, acc_ref):
        def step(k, carry):
            pair = [jnp.concatenate([r[2 * k + j, 0] for r in parts], axis=0) for j in range(2)]
            acc_ref[...] += rows_gram(jnp.concatenate(pair, axis=1))
            return carry

        lax.fori_loop(0, nx // 2, step, 0)

    def finish(acc_ref, mine, o_refs, e_ref):
        r = lax.broadcasted_iota(jnp.int32, (n, n), 0)
        c = lax.broadcasted_iota(jnp.int32, (n, n), 1)
        select = jnp.where(r == ((c // no) ^ mine) * no + c % no, 1.0, 0.0).astype(F32)
        full = exact_nt(symmetric(acc_ref[...], n), select)
        for d in range(sources):
            o_refs[d][:no] = full[d * no : (d + 1) * no]
            o_refs[d][no:] = e_ref[...]

    outs = [(no + extra.shape[0], n)] * sources if last else [(n, 2 * n)]
    finish, extra = (finish, (extra,)) if last else (None, ())
    return gram_parts(add, finish, own, base, received, place, prev, n, outs, extra)


def project(own, base, received, first, slots, factor_in, turned_out, prev):
    nx, count, no, ni = received[0].shape
    sources = len(received) + 1
    ra = factor_in.shape[1]
    nb = turned_out.shape[0] // sources
    n_prev = 0 if prev is None else sources

    def kernel(s_ref, own_ref, *refs):
        parts = (own_ref, *refs[: sources - 1])
        in_ref, out_ref = refs[sources - 1 : sources + 1]
        v_refs = refs[sources + 1 + n_prev :]
        in_high, in_low = split(in_ref[...])
        in_both = jnp.concatenate([in_high, in_low], axis=1)
        out_high, out_low = split(out_ref[...])

        def step(x, carry):
            high, low = split(jnp.concatenate([r[x, 0] for r in parts], axis=0))
            u = dot_nn(high, in_both)
            u = u[:, :ra] + (u[:, ra:] + dot_nn(low, in_high))
            u_high, u_low = split(u)
            v = dot_nn(out_high, jnp.concatenate([u_high, u_low], axis=1))
            v = v[:, :ra] + (v[:, ra:] + dot_nn(out_low, u_high))
            for d in range(sources):
                v_refs[d][x, 0] = v[d * nb : (d + 1) * nb]
            return carry

        lax.fori_loop(0, nx, step, 0)

    grid_spec = pltpu.PrefetchScalarGridSpec(
        num_scalar_prefetch=1,
        grid=(count,),
        in_specs=[pl.BlockSpec((nx, 1, no, ni), lambda u, s: (0, s[0] + u, 0, 0))]
        + [pl.BlockSpec((nx, 1, no, ni), lambda u, s: (0, u, 0, 0))] * (sources - 1)
        + [
            pl.BlockSpec(factor_in.shape, lambda u, s: (0, 0)),
            pl.BlockSpec(turned_out.shape, lambda u, s: (0, 0)),
        ]
        + [pl.BlockSpec(memory_space=pl.ANY)] * n_prev,
        out_specs=[pl.BlockSpec((nx, 1, nb, ra), lambda u, s: (0, first + u, 0, 0))] * sources,
    )
    return pl.pallas_call(
        kernel,
        grid_spec=grid_spec,
        out_shape=[jax.ShapeDtypeStruct((nx, slots, nb, ra), F32)] * sources,
        input_output_aliases={sources + 3 + d: d for d in range(n_prev)},
        compiler_params=LIMITED,
        name="project",
    )(jnp.stack([base]).astype(jnp.int32), own, *received, factor_in, turned_out, *(prev or ()))


def contract_y(parts, place, factor_y, nc):
    nx, count, nb, na = parts[0].shape
    _, nq = factor_y.shape
    sources = len(parts)
    x_step = 4 if nx % 4 == 0 else nx
    q_step = 2 if nq % 2 == 0 else 1

    def kernel(s_ref, f_ref, *refs):
        o_ref = refs[sources]
        mine = s_ref[0]
        for q0 in range(0, nq, q_step):
            totals = {}
            for r in range(sources):
                for u in range(count):
                    slot = (mine ^ r) * count + u
                    scales = [f_ref[slot // nc, q0 + j] for j in range(q_step)]
                    for x in range(x_step):
                        value = refs[r][x, u]
                        for j in range(q_step):
                            term = scales[j] * value
                            for c in range(nc):
                                if count % nc == 0:
                                    if u % nc != c:
                                        continue
                                    part = term
                                else:
                                    part = jnp.where(slot % nc == c, term, 0.0)
                                key = (j, x, c)
                                totals[key] = totals[key] + part if key in totals else part
            for (j, x, c), total in totals.items():
                o_ref[x, :, (q0 + j) * nc + c, :] = total

    return pl.pallas_call(
        kernel,
        grid=(nx // x_step,),
        in_specs=[
            pl.BlockSpec(memory_space=pltpu.SMEM),
            pl.BlockSpec(memory_space=pltpu.SMEM),
        ]
        + [pl.BlockSpec((x_step, count, nb, na), lambda x: (x, 0, 0, 0))] * sources,
        out_specs=pl.BlockSpec((x_step, nb, nq * nc, na), lambda x: (x, 0, 0, 0)),
        out_shape=jax.ShapeDtypeStruct((nx, nb, nq * nc, na), F32),
        compiler_params=LIMITED,
        name="contract_y",
    )(jnp.stack([place]).astype(jnp.int32), factor_y, *parts)


def contract_x(parts, place, factor_x):
    nx, rows, na = parts[0].shape
    sources = len(parts)
    parts = [pltpu.with_memory_space_constraint(part, pltpu.VMEM) for part in parts]
    np_ = factor_x.shape[1] // sources

    def kernel(s_ref, f_ref, *refs):
        mine = s_ref[0]
        for d in range(sources):
            totals = [None] * np_
            for r in range(sources):
                for x in range(nx):
                    value = refs[r][x]
                    for p in range(np_):
                        scale = f_ref[(mine ^ r) * nx + x, (mine ^ d) * np_ + p]
                        term = scale * value
                        totals[p] = term if totals[p] is None else totals[p] + term
            for p in range(np_):
                refs[sources + d][p] = totals[p]

    return pl.pallas_call(
        kernel,
        in_specs=[
            pl.BlockSpec(memory_space=pltpu.SMEM),
            pl.BlockSpec(memory_space=pltpu.SMEM),
        ]
        + [pl.BlockSpec(memory_space=pltpu.VMEM)] * sources,
        out_specs=[pl.BlockSpec(memory_space=pltpu.VMEM)] * sources,
        out_shape=[jax.ShapeDtypeStruct((np_, rows, na), F32)] * sources,
        compiler_params=LIMITED,
        name="contract_x",
    )(jnp.stack([place]).astype(jnp.int32), factor_x, *parts)


def assemble(parts, place):
    parts = [pltpu.with_memory_space_constraint(part, pltpu.VMEM) for part in parts]
    sources = len(parts)
    np_, rows, na = parts[0].shape

    def kernel(s_ref, *refs):
        for r in range(sources):
            refs[sources][:, s_ref[0] ^ r] = refs[r][...]

    return pl.pallas_call(
        kernel,
        in_specs=[pl.BlockSpec(memory_space=pltpu.SMEM)]
        + [pl.BlockSpec(memory_space=pltpu.VMEM)] * sources,
        out_specs=pl.BlockSpec(memory_space=pltpu.VMEM),
        out_shape=jax.ShapeDtypeStruct((np_, sources, rows, na), F32),
        compiler_params=LIMITED,
        name="assemble",
    )(jnp.stack([place]).astype(jnp.int32), *parts)


def splat(value, i, k):
    column = jnp.broadcast_to(value[:, k : k + 1], value.shape)
    return jnp.broadcast_to(column[i : i + 1, :], value.shape)


def inverse_factor(d):
    scale = [None] * ROWS
    lower = [[None] * ROWS for _ in range(ROWS)]
    for k in range(ROWS):
        y = lax.rsqrt(d[k][k])
        scale[k] = y * (1.5 - 0.5 * d[k][k] * y * y)
        for i in range(k + 1, ROWS):
            lower[i][k] = d[i][k] * scale[k]
        for j in range(k + 1, ROWS):
            for i in range(j, ROWS):
                d[i][j] = d[i][j] - lower[i][k] * lower[j][k]
    inverse = [[None] * ROWS for _ in range(ROWS)]
    for k in range(ROWS):
        inverse[k][k] = scale[k]
        for i in range(k + 1, ROWS):
            total = lower[i][k] * inverse[k][k]
            for j in range(k + 1, i):
                total = total + lower[i][j] * inverse[j][k]
            inverse[i][k] = -scale[i] * total
    return inverse


def panel(r, rolled, e):
    row = lax.broadcasted_iota(jnp.int32, r.shape, 0)
    d = [[splat(rolled, i, k) if i >= k else None for k in range(ROWS)] for i in range(ROWS)]
    inverse = inverse_factor(d)
    upper = jnp.zeros_like(r)
    out = jnp.zeros_like(e)
    for k in range(ROWS):
        column = jnp.zeros_like(r)
        for i in range(k, ROWS):
            column = jnp.where(row == i, inverse[i][k], column)
        upper = upper + column * jnp.broadcast_to(r[k : k + 1, :], r.shape)
        out = out + column * jnp.broadcast_to(e[k : k + 1, :], e.shape)
    return upper, out


def trailing(a_ref, e_ref, upper, out, turned, first, stop):
    shape = upper.shape
    upper_rows = [jnp.broadcast_to(upper[k : k + 1, :], shape) for k in range(ROWS)]
    out_rows = [jnp.broadcast_to(out[k : k + 1, :], shape) for k in range(ROWS)]
    for q in range(first, stop):
        here = slice(q * ROWS, (q + 1) * ROWS)
        a_part = jnp.zeros_like(upper)
        e_part = jnp.zeros_like(out)
        for k in range(ROWS):
            column = jnp.broadcast_to(turned[here, k : k + 1], shape)
            a_part = a_part + column * upper_rows[k]
            e_part = e_part + column * out_rows[k]
        a_ref[here, :] = a_ref[here, :] - a_part
        e_ref[here, :] = e_ref[here, :] - e_part


def invert_lower(a_ref, e_ref):
    n = a_ref.shape[0]
    i = lax.broadcasted_iota(jnp.int32, (n, n), 0)
    k = lax.broadcasted_iota(jnp.int32, (n, n), 1)
    e_ref[...] = jnp.where(i == k, 1.0, 0.0).astype(F32)
    groups = n // ROWS
    if n % 128:
        for p in range(groups):
            here = slice(p * ROWS, (p + 1) * ROWS)
            r = a_ref[here, :]
            rolled = r
            if p:
                rolled = jnp.concatenate([r[:, p * ROWS :], r[:, : p * ROWS]], axis=1)
            upper, out = panel(r, rolled, e_ref[here, :])
            e_ref[here, :] = out
            if p + 1 < groups:
                trailing(a_ref, e_ref, upper, out, upper.T, p + 1, groups)
        return

    def step(p, carry):
        start = pl.multiple_of(p * ROWS, ROWS)
        r = a_ref[pl.ds(start, ROWS), :]
        rolled = pltpu.roll(r, (n - start) % n, 1)
        upper, out = panel(r, rolled, e_ref[pl.ds(start, ROWS), :])
        e_ref[pl.ds(start, ROWS), :] = out
        turned = upper.T
        row = lax.broadcasted_iota(jnp.int32, turned.shape, 0)
        turned = jnp.where(row >= start + ROWS, turned, 0.0)
        trailing(a_ref, e_ref, upper, out, turned, 0, groups)
        return carry

    lax.fori_loop(0, groups, step, 0)


def sweeps(parts, start, turned=(False,) * SWEEPS, place=None, cuts=1, keep=None):
    n, ranks = start.shape
    count = len(parts)
    size = ranks // cuts
    n_out = 1 if place is None else 2

    def kernel(place_ref, *refs):
        s_ref = refs[count]
        outs = refs[count + 1 : count + 1 + n_out]
        a_ref, e_ref = refs[count + 1 + n_out :]
        gram = jnp.concatenate([r[:keep] for r in refs[:count]], axis=0)
        subspace = s_ref[...]
        for turn in turned:
            product = exact_tn(gram, subspace) if turn else exact_nn(gram, subspace)
            a_ref[...] = exact_tn(product, product)
            invert_lower(a_ref, e_ref)
            subspace = exact_nt(product, e_ref[...])
        outs[0][...] = subspace
        if place is not None:
            mine = place_ref[0]
            r = lax.broadcasted_iota(jnp.int32, (ranks, ranks), 0)
            c = lax.broadcasted_iota(jnp.int32, (ranks, ranks), 1)
            select = jnp.where(c == ((r // size) ^ mine) * size + r % size, 1.0, 0.0).astype(F32)
            outs[1][...] = exact_nt(exact_nn(select, e_ref[...]), product)

    return pl.pallas_call(
        kernel,
        in_specs=[pl.BlockSpec(memory_space=pltpu.SMEM)]
        + [pl.BlockSpec(memory_space=pltpu.VMEM)] * (count + 1),
        out_specs=[pl.BlockSpec(memory_space=pltpu.VMEM)] * n_out,
        out_shape=[jax.ShapeDtypeStruct((n, ranks), F32), jax.ShapeDtypeStruct((ranks, n), F32)][
            :n_out
        ],
        scratch_shapes=[pltpu.VMEM((ranks, ranks), F32)] * 2,
        compiler_params=LIMITED,
        name="sweeps",
    )(jnp.stack([0 if place is None else place]).astype(jnp.int32), *parts, start)


def swap(value, axis, s):
    n = lax.axis_size(axis)
    return lax.ppermute(value, axis, [(i, i ^ s) for i in range(n)])


def total_over(value, axis):
    n = lax.axis_size(axis)
    base = 1
    while base < n:
        group = min(4, n // base)
        arrived = [swap(value, axis, base * k) for k in range(1, group)]
        for other in arrived:
            value = value + other
        base *= group
    return value


def block(value, index, size, dim):
    return lax.dynamic_slice_in_dim(value, index * size, size, dim)


def pieces(count, shares):
    runs = []
    start = 0
    total = sum(shares)
    seen = 0
    for share in shares:
        seen += share
        stop = (count * seen) // total
        if stop > start:
            runs.append((start, stop - start))
            start = stop
    return runs


def all_but(value, axis):
    return [swap(value, axis, s) for s in range(1, lax.axis_size(axis))]


def added(values):
    total = values[0]
    for value in values[1:]:
        total = total + value
    return total


def relative_rows(value, place, count):
    size = value.shape[0] // count
    return jnp.concatenate([block(value, place ^ s, size, 0) for s in range(count)], axis=0)


def shards(gradient, start_in, start_out, start_x, start_y):
    f = lax.axis_index("fsdp")
    m = lax.axis_index("mode")
    joint = lax.axis_index(("fsdp", "mode"))
    nf = lax.axis_size("fsdp")
    nm = lax.axis_size("mode")
    nx, ny, nc, no, ni = gradient.shape
    slots = ny * nc
    flat = gradient.reshape(nx, slots, no, ni)
    per_mode = slots // nm
    per_fsdp = slots // nf

    def cut(place, count, per, run, after=None):
        source = flat if after is None else lax.optimization_barrier((flat, after))[0]
        return [
            lax.dynamic_slice(source, (0, (place ^ s) * per + run[0], 0, 0), (nx, run[1], no, ni))
            for s in range(1, count)
        ]

    def exchange(axis, parts):
        arrived = []
        for s, part in enumerate(parts):
            arrived.append(swap(part, axis, s + 1))
        return arrived

    mode_runs = pieces(per_mode, (2, 1, 1, 1, 1, 2))
    fsdp_runs = pieces(per_fsdp, (1, 3))

    def cut_mode(k, after=None):
        return cut(m, nm, per_mode, mode_runs[k], after)

    def cut_fsdp(k, after=None):
        return cut(f, nf, per_fsdp, fsdp_runs[k], after)

    mode_cuts = [cut_mode(0)]
    fsdp_cuts = [cut_fsdp(0, mode_cuts[0][0])]
    for k in range(1, len(fsdp_runs)):
        fsdp_cuts.append(cut_fsdp(k, fsdp_cuts[0][0]))
    for k in range(1, len(mode_runs)):
        mode_cuts.append(cut_mode(k, fsdp_cuts[-1][0]))
    mode_parts = []
    for parts in mode_cuts:
        mode_parts.append(exchange("mode", parts))
    fsdp_parts = []
    for parts in fsdp_cuts:
        fsdp_parts.append(exchange("fsdp", parts))

    source = lax.optimization_barrier((gradient, fsdp_cuts[0][0]))[0]
    gram_y = gram_y_part(source)
    groups_y = range(0, ny, ROWS)
    folded_y = jnp.concatenate([gram_y[k : k + ROWS] for k in groups_y], axis=1)
    folded_y = jnp.pad(folded_y, ((0, 0), (0, nf * no - folded_y.shape[1])))
    rows = source.reshape(nx * slots * no, ni)
    gram_in = lax.dot_general(rows, rows, (((0,), (0,)), ((), ())), precision=lax.Precision.HIGH)

    rows_in = ni // nf
    messages = [block(gram_in, f ^ s, rows_in, 0) for s in range(nf)]
    arrived = [swap(messages[s], "fsdp", s) for s in range(1, nf)]
    sum_in = added([messages[0]] + arrived)
    kept, sent = (block(sum_in, (m & 1) ^ s, rows_in // 2, 0) for s in range(2))
    sum_in = kept + swap(sent, "mode", 1)
    s = 2
    while s < nm:
        sum_in = sum_in + swap(sum_in, "mode", s)
        s *= 2
    sum_in = jnp.concatenate([sum_in, swap(sum_in, "mode", 1)], axis=0)
    gathered = [sum_in] + all_but(sum_in, "fsdp")
    (full_in,) = sweeps(gathered, start_in, (False, True))

    gram_out = [None]
    for k, (run, parts) in enumerate(zip(fsdp_runs, fsdp_parts)):
        last = k == len(fsdp_runs) - 1
        base = f * per_fsdp + run[0]
        gram_out = gram_out_part(flat, base, parts, f, gram_out[0], last, folded_y)
    sum_out = added([gram_out[0]] + [swap(gram_out[s], "fsdp", s) for s in range(1, nf)])
    sum_out = added([sum_out] + all_but(sum_out, "mode"))
    folded_y = sum_out[no:]
    gram_y = jnp.concatenate(
        [folded_y[:, k // ROWS * ny : (k // ROWS + 1) * ny] for k in groups_y], axis=0
    )
    (factor_y,) = sweeps([gram_y], start_y)
    sum_out = sum_out[:no]
    gathered = [sum_out] + all_but(sum_out, "fsdp")
    full_out, turned_out = sweeps(gathered, relative_rows(start_out, f, nf), (True, False), f, nf)

    by_b = None
    for run, parts in zip(fsdp_runs, fsdp_parts):
        base = f * per_fsdp + run[0]
        by_b = project(flat, base, parts, run[0], per_fsdp, full_in, turned_out, by_b)
    by_b = [by_b[0]] + [swap(by_b[s], "fsdp", s) for s in range(1, nf)]
    reduced = contract_y(by_b, f, factor_y, nc)
    nb, na = reduced.shape[1], reduced.shape[3]
    reduced = reduced.reshape(nx, -1, na)
    nr = reduced.shape[1] // nm

    gram_x = None
    for k, (run, parts) in enumerate(zip(mode_runs, mode_parts)):
        last = k == len(mode_runs) - 1
        gram_x = gram_x_part(flat, m * per_mode + run[0], parts, m, gram_x, last)
    gram_x = total_over(gram_x, "mode")
    gram_x = total_over(gram_x, "fsdp")
    by_x = [block(reduced, m ^ s, nr, 1) for s in range(nm)]
    by_x = by_x[:1] + [swap(by_x[s], "mode", s) for s in range(1, nm)]
    (factor_x,) = sweeps([gram_x], start_x)
    by_p = contract_x(by_x, m, factor_x)
    by_p = [by_p[0]] + exchange("mode", by_p[1:])
    core = assemble(by_p, m)
    core = core.reshape(core.shape[0], nb, -1, nc, na)

    rows_in = ni // (nf * nm)
    factor_in = block(full_in, joint, rows_in, 0)
    return (factor_in, full_out[:no], factor_x, factor_y, core)


def solution(mesh):
    in_specs = (P("mode", None, None, "fsdp", None), P(), P(), P(), P())
    out_specs = (
        P(("fsdp", "mode"), None),
        P("fsdp", None),
        P(),
        P(),
        P("mode", "fsdp", None, None, None),
    )
    return jax.shard_map(shards, mesh=mesh, in_specs=in_specs, out_specs=out_specs, check_vma=False)
```
